32 devices in a mesh: wide: 4 (over y, core), narrow: 8 (over z, x).
Axes of the slice: x: 2, y: 2, z: 4, core: 2. Of those that a mesh axis runs over, the one named last changes fastest.
Arguments:
- inputs: bfloat16 [64, 1024, 512], P('narrow', 'wide'), may hold values from -6 to 6
- conv_w: bfloat16 [9, 512, 512], replicated, may hold values from -0.09375 to 0.09375
- conv_b: bfloat16 [512], replicated, may hold values from -3 to 3
- ln1_gain: bfloat16 [512], replicated, may hold values from 0.25 to 1.75
- ln1_bias: bfloat16 [512], replicated, may hold values from -2 to 2
- w_in: bfloat16 [512, 2048], replicated, may hold values from -0.25 to 0.25
- b_in: bfloat16 [2048], replicated, may hold values from -3 to 3
- w_out: bfloat16 [2048, 512], replicated, may hold values from -0.125 to 0.125
- ln2_gain: bfloat16 [512], replicated, may hold values from 0.25 to 1.75
- ln2_bias: bfloat16 [512], replicated, may hold values from -2 to 2
- segments: int32 [64, 1024], P('narrow', 'wide'), may hold values from 0 to 7, never falling along the last dimension, each value on 1 to 512 neighbouring positions
- tap_mask: int32 [64, 9, 1024], P('narrow', None, 'wide'), may hold values 0 or 1
- cotangent: bfloat16 [64, 1024, 512], P('narrow', 'wide'), may hold values from -6 to 6
Outputs:
- out: bfloat16 [64, 1024, 512], P('narrow', 'wide')
- grad_inputs: float32 [64, 1024, 512], P('narrow', 'wide')
- grad_conv_w: float32 [9, 512, 512], P(None, 'narrow', 'wide')
- grad_conv_b: float32 [512], replicated
- grad_ln1_gain: float32 [512], replicated
- grad_ln1_bias: float32 [512], replicated
- grad_w_in: float32 [512, 2048], P('narrow', 'wide')
- grad_b_in: float32 [2048], replicated
- grad_w_out: float32 [2048, 512], P('narrow', 'wide')
- grad_ln2_gain: float32 [512], replicated
- grad_ln2_bias: float32 [512], replicated
The draws below stay inside these ranges and needn't reach their ends.
Inputs may be any that keep to these rules, and one draw needn't show every extreme that they name: `segments`: ids never fall along a row; one id covers at most 512 positions of a row, and some id exactly that many.
All inputs are finite; a program needn't handle non-finite values. No bound on the sum of `tap_mask` on one device may be relied on, other than what follows from the above.
Results may differ from the reference program's by a relative error of at most 0.0073.
Values may be sent and summed in bfloat16 or wider, within the bound.
No kernel may reach another device: no remote copies, remote signals or barrier semaphores. Data moves between devices by JAX's collectives and lax.ppermute only.
A program may use at most 256 MiB of HBM per device.

```python
import math
import jax
import jax.numpy as jnp
import numpy as np
from jax import lax

D = 512
FF = 2048
KERNEL_TAPS = 9
DILATION_STEP = 32
ROWS = 64
ROW_LENGTH = 1024


def set_ends(values, key, low, largest):
    dims = values.shape
    spot = [jax.random.randint(jax.random.fold_in(key, axis), (), 0, dims[axis]) for axis in range(len(dims))]
    values = values.at[tuple(spot)].set(low)
    longest = dims.index(max(dims))
    spot[longest] = (spot[longest] + 1) % dims[longest]
    return values.at[tuple(spot)].set(largest)


def strengthened(values, own_key, source, target, parts, factor):
    owner, partner = [(jnp.arange(values.shape[dim]) // (values.shape[dim] // parts)).reshape([-1 if axis == dim else 1 for axis in range(values.ndim)]) for dim in (source, target)]
    chosen = jax.random.permutation(own_key, parts)[partner]
    strong = (owner == chosen) | (owner == (partner + parts // 2) % parts)
    return jnp.where(strong, factor * values, values)


def level_of(own_key, extent, shards, smallest, top_value):
    level, own = 1.0, jax.random.fold_in(own_key, 6)
    for axis_at, blocks in shards:
        draws = jnp.exp(jax.random.uniform(jax.random.fold_in(own, axis_at), (blocks,), jnp.float32, smallest / len(shards), top_value / len(shards)))
        level = level * jnp.repeat(draws, extent[axis_at] // blocks).reshape([-1 if axis == axis_at else 1 for axis in range(len(extent))])
    return level


def split_up(count, total, reach, slope):
    loads = [(1 << 20) // math.isqrt(standing ** slope) + 1 for standing in range(2, count + 1)]
    spare, counts = total - reach - (count - 1), [1] * (count - 1)
    while spare > 0:
        candidates = [i for i in range(count - 1) if counts[i] < reach]
        whole, budget = sum([loads[i] for i in candidates]), spare
        for i in candidates:
            addition = min(reach - counts[i], max(1, budget * loads[i] // whole), spare)
            counts[i] = counts[i] + addition
            spare = spare - addition
    return np.array([reach] + counts)


def uneven(key, amount, total, most, lean):
    if amount == 2:
        one = jax.random.randint(key, (), max(1, total - most), min(most, total - 1) + 1)
        return jnp.stack([one, total - one])
    tallies = jnp.asarray(split_up(amount, total, most, lean), jnp.int32)
    pairs = (amount - 1) // 2
    giver, taker = tallies[1:1 + 2 * pairs:2], tallies[2:2 + 2 * pairs:2]
    margin = jnp.minimum(giver - 1, most - taker)
    shifted = jax.random.randint(jax.random.fold_in(key, 1), (pairs,), 0, 1 << 20) % (margin + 1)
    tallies = tallies.at[1:1 + 2 * pairs:2].set(giver - shifted).at[2:2 + 2 * pairs:2].set(taker + shifted)
    return tallies[jax.random.permutation(jax.random.fold_in(key, 2), amount)]


def gaussian(rng, shape, scale, reach, cuts=(), dtype=jnp.bfloat16):
    array = scale * jax.random.normal(rng, shape, jnp.float32)
    if cuts:
        array = array * level_of(rng, shape, cuts, -0.22, 0.18)
    return jnp.clip(array, -reach, reach).astype(dtype)


def heavy_noise(key, shape, width, reach, cuts, heavy, kind=jnp.bfloat16):
    entries = width * jax.random.normal(key, shape, jnp.float32)
    if cuts:
        entries = entries * level_of(key, shape, cuts, -0.22, 0.18)
    return jnp.clip(strengthened(entries, jax.random.fold_in(key, 3), *heavy), -reach, reach).astype(kind)


def setup_inputs(seed: int = 0) -> dict:
    keys = jax.random.split(jax.random.key(seed), 14)
    inputs = gaussian(keys[0], (ROWS, ROW_LENGTH, D), 1.0, 6.0, ((0, 8), (1, 4)))
    conv_w = gaussian(keys[1], (KERNEL_TAPS, D, D), (KERNEL_TAPS * D) ** -0.5, 0.09375)
    conv_b = gaussian(keys[2], (D,), 0.5, 3.0)
    ln1_gain = jnp.clip(1.0 + 0.15 * jax.random.normal(keys[3], (D,), jnp.float32), 0.25, 1.75).astype(jnp.bfloat16)
    ln1_bias = gaussian(keys[4], (D,), 0.3, 2.0)
    w_in = gaussian(keys[5], (D, FF), D ** -0.5, 0.25)
    b_in = gaussian(keys[6], (FF,), 0.5, 3.0)
    w_out = gaussian(keys[7], (FF, D), FF ** -0.5, 0.125)
    ln2_gain = jnp.clip(1.0 + 0.15 * jax.random.normal(keys[8], (D,), jnp.float32), 0.25, 1.75).astype(jnp.bfloat16)
    ln2_bias = gaussian(keys[9], (D,), 0.3, 2.0)
    segments = jax.vmap(lambda own: jnp.searchsorted(jnp.cumsum(uneven(own, ROW_LENGTH // 128, ROW_LENGTH, ROW_LENGTH // 2, 0)), jnp.arange(ROW_LENGTH), side="right"))(jax.random.split(keys[10], ROWS)).reshape((ROWS, ROW_LENGTH)).astype(jnp.int32)
    tap_mask = set_ends((jax.random.randint(keys[11], (ROWS, KERNEL_TAPS, ROW_LENGTH), 0, 8) < 7).astype(jnp.int32), jax.random.fold_in(keys[11], 1), 0, 1)
    cotangent = heavy_noise(keys[12], (ROWS, ROW_LENGTH, D), 1.0, 6.0, ((0, 8), (1, 4)), (1, 2, 4, 2.0))
    return {"inputs": inputs, "conv_w": conv_w, "conv_b": conv_b, "ln1_gain": ln1_gain, "ln1_bias": ln1_bias, "w_in": w_in, "b_in": b_in, "w_out": w_out, "ln2_gain": ln2_gain, "ln2_bias": ln2_bias, "segments": segments, "tap_mask": tap_mask, "cotangent": cotangent}


@jax.custom_vjp
def low(v):
    return lax.optimization_barrier(v.astype(jnp.bfloat16)).astype(jnp.float32)

@jax.custom_vjp
def low_back(v):
    return v

def low_keep(v):
    return (low(v), None)

def low_pass(kept, grad):
    return (grad,)

def back_keep(v):
    return (v, None)

def back_low(kept, grad):
    return (low(grad),)
low.defvjp(low_keep, low_pass)
low_back.defvjp(back_keep, back_low)

def layer_norm(values, gain_vec, bias_vec):
    centre = lax.optimization_barrier(jnp.mean(values, axis=-1, keepdims=True))
    centered = values - centre
    spread = lax.optimization_barrier(jnp.mean(centered * centered, axis=-1, keepdims=True))
    return centered * lax.rsqrt(spread + 1e-05) * gain_vec + bias_vec

def tap_validity(seg_rows, mask_rows):
    tap_distance = DILATION_STEP * (KERNEL_TAPS // 2)
    padded_input = jnp.pad(seg_rows, ((0, 0), (tap_distance, tap_distance)), constant_values=-1)
    tap_list = []
    for tap_number in range(KERNEL_TAPS):
        source_rows = padded_input[:, tap_number * DILATION_STEP:tap_number * DILATION_STEP + ROW_LENGTH]
        matched = (source_rows == seg_rows) & (mask_rows[:, tap_number, :] == 1)
        tap_list.append(jnp.where(matched, 1.0, 0.0))
    return jnp.stack(tap_list, axis=1).astype(jnp.float32)

def layer_forward(x_value, params, validity_mask):
    conv_w, conv_b, gain_one, bias_one, w_in, b_in, w_out, gain_two, bias_two = params
    highest = lax.Precision.HIGHEST
    conv_in = low_back(low(x_value))
    tap_distance = DILATION_STEP * (KERNEL_TAPS // 2)
    padded_input = jnp.pad(conv_in, ((0, 0), (tap_distance, tap_distance), (0, 0)))
    summed = jnp.zeros(x_value.shape, jnp.float32)
    for tap_number in range(KERNEL_TAPS):
        source_rows = padded_input[:, tap_number * DILATION_STEP:tap_number * DILATION_STEP + ROW_LENGTH, :] * validity_mask[:, tap_number, :, None]
        summed = summed + jnp.einsum('gpc,cd->gpd', source_rows, conv_w[tap_number], precision=highest)
    hidden = low_back(low(summed + conv_b))
    mixed_rows = x_value + layer_norm(jax.nn.gelu(hidden, approximate=False), gain_one, bias_one)
    mixed_low = low(mixed_rows)
    up_value = low_back(jnp.einsum('gpd,df->gpf', mixed_low, w_in, precision=highest) + b_in)
    act_low = low(jax.nn.gelu(up_value, approximate=False))
    projected = low_back(jnp.einsum('gpf,fd->gpd', act_low, w_out, precision=highest))
    return mixed_rows + layer_norm(projected, gain_two, bias_two)

def reference(inputs, conv_w, conv_b, ln1_gain, ln1_bias, w_in, b_in, w_out, ln2_gain, ln2_bias, segments, tap_mask, cotangent):
    weights = (conv_w.astype(jnp.float32), conv_b.astype(jnp.float32), ln1_gain.astype(jnp.float32), ln1_bias.astype(jnp.float32), w_in.astype(jnp.float32), b_in.astype(jnp.float32), w_out.astype(jnp.float32), ln2_gain.astype(jnp.float32), ln2_bias.astype(jnp.float32))
    group_rows = math.gcd(ROWS, max(1, 4096 // ROW_LENGTH))
    batches = ROWS // group_rows

    def one_group(running, pieces):
        x_part, seg_part, mask_part, ct_part = pieces
        validity_mask = tap_validity(seg_part, mask_part)

        def forward(x_value, params):
            return layer_forward(x_value, params, validity_mask)
        result, pullback = jax.vjp(forward, x_part.astype(jnp.float32), weights)
        grad_x, grad_params = pullback(ct_part.astype(jnp.float32))
        running = jax.tree.map(lambda total_part, added: total_part + added, running, grad_params)
        return (running, (result.astype(jnp.bfloat16), grad_x))
    initial = jax.tree.map(jnp.zeros_like, weights)
    pieces = (inputs.reshape(batches, group_rows, ROW_LENGTH, D), segments.reshape(batches, group_rows, ROW_LENGTH), tap_mask.reshape(batches, group_rows, KERNEL_TAPS, ROW_LENGTH), cotangent.reshape(batches, group_rows, ROW_LENGTH, D))
    summed, (outputs, grads_x) = lax.scan(one_group, initial, pieces)
    return (outputs.reshape(ROWS, ROW_LENGTH, D), grads_x.reshape(ROWS, ROW_LENGTH, D), summed[0], summed[1], summed[2], summed[3], summed[4], summed[5], summed[6], summed[7], summed[8])
```

```python
import functools

import jax
import jax.numpy as jnp
from jax import lax
from jax.experimental import pallas as pl
from jax.experimental.pallas import tpu as pltpu
from jax.sharding import PartitionSpec as P

STEP = 32
BF = jnp.bfloat16
F32 = jnp.float32
RSQRT2 = 0.7071067811865476
RSQRT2PI = 0.3989422804014327
EPS = 1e-05
VMEM_LIMIT = 56 * 1024 * 1024


def params():
    return pltpu.CompilerParams(vmem_limit_bytes=VMEM_LIMIT)


def cost(flops, moved, transcendentals=0):
    return pl.CostEstimate(
        flops=int(flops), bytes_accessed=int(moved), transcendentals=int(transcendentals)
    )


def whole(shape):
    rank = len(shape)
    return pl.BlockSpec(shape, lambda *_: (0,) * rank, pipeline_mode=pl.Buffered(1))


def shape(dims, dtype):
    return jax.ShapeDtypeStruct(dims, dtype)


def mask_columns(matched):
    return jnp.where(matched, 1.0, 0.0).astype(F32).T


def spread(column, width):
    wide = jnp.broadcast_to(column, (column.shape[0], 128)).astype(BF)
    return jnp.concatenate([wide] * (width // 128), axis=1)


def dot(left, right, left_dim, right_dim):
    return lax.dot_general(
        left, right, (((left_dim,), (right_dim,)), ((), ())), preferred_element_type=F32
    )


def cdf_and_exp(values):
    return 0.5 + 0.5 * lax.erf(values * RSQRT2), jnp.exp(-0.5 * values * values)


def fold(values):
    return values.reshape(-1, 8, values.shape[-1]).sum(0)


def conv_inner_kernel(info_ref, x_ref, w_ref, acc_ref):
    tap = pl.program_id(0)
    rows, own, features = x_ref.shape
    taps = info_ref.shape[0] - 1
    half = taps // 2
    ids = info_ref[0]

    def run(k):
        shift = STEP * (k - half)
        low, high = max(0, -shift), own - max(0, shift)
        matched = (ids[:, low + shift : high + shift] == ids[:, low:high]) & (
            info_ref[1 + k][:, low:high] == 1
        )
        columns = mask_columns(matched)
        lhs = jnp.concatenate(
            [
                x_ref[r, low + shift : high + shift, :] * spread(columns[:, r : r + 1], features)
                for r in range(rows)
            ],
            axis=0,
        )
        product = dot(lhs, w_ref[0], 1, 0).reshape(rows, high - low, features)
        if k == half:
            acc_ref[...] = product
        else:
            acc_ref[:, low:high, :] += product

    for k in range(taps):
        place = 0 if k == half else (k + 1 if k < half else k)
        pl.when(tap == place)(functools.partial(run, k))


def conv_inner(info, x, conv_w):
    rows, own, features = x.shape
    taps = conv_w.shape[0]
    half = taps // 2

    def tap_of(i):
        return jnp.where(i == 0, half, jnp.where(i <= half, i - 1, i))

    return pl.pallas_call(
        conv_inner_kernel,
        grid=(taps,),
        in_specs=[
            whole(info.shape),
            whole(x.shape),
            pl.BlockSpec((1, features, features), lambda i: (tap_of(i), 0, 0)),
        ],
        out_specs=whole(x.shape),
        out_shape=shape(x.shape, F32),
        compiler_params=params(),
        cost_estimate=cost(2 * rows * own * features * features * taps * 0.72, 11e6),
        name="conv_inner",
    )(info, x, conv_w)


def place_block(out_ref, value, dest_wide, dest_narrow, rows_at, blocks):
    if blocks == (1, 1):
        out_ref[0, 0, rows_at, :] = value
        return
    rel_wide = lax.axis_index("wide") ^ dest_wide
    rel_narrow = lax.axis_index("narrow") ^ dest_narrow
    index = (rel_wide >> 1) * 8 + (rel_narrow & 1) * 4 + (rel_narrow >> 1)
    out_ref[rel_wide & 1, index, rows_at, :] = value


def ship(scratch, keep_ref, send_ref, sems):
    first = pltpu.make_async_copy(scratch.at[0], keep_ref, sems.at[0])
    second = pltpu.make_async_copy(scratch.at[1], send_ref, sems.at[1])
    first.start()
    second.start()
    first.wait()
    second.wait()


def forward_kernel(
    blocks,
    info_ref, acc_ref, left_ref, right_ref, x_ref, ct_ref, conv_w_ref, w_in_ref, w_out_ref,
    vec_ref, b_in_ref,
    out_ref, low_ref, hidden_ref, gproj_ref, slope_ref, gain_ref, bias_ref, *rest,
):
    if blocks == (1, 1):
        gw_ref, halo_acc, act_scr, gp_scr = rest
    else:
        keep_ref, send_ref, halo_acc, act_scr, gp_scr, gw_ref, sems = rest
    step = pl.program_id(0)
    steps = pl.num_programs(0)
    rows, own, features = halo_acc.shape
    taps = info_ref.shape[0] - 1
    half = taps // 2
    reach = STEP * half
    block_rows = x_ref.shape[0]
    size = block_rows * own
    hidden_units = w_in_ref.shape[1]

    @pl.when(step == 0)
    def _():
        gain_ref[...] = jnp.zeros_like(gain_ref)
        bias_ref[...] = jnp.zeros_like(bias_ref)
        ids = info_ref[0]
        for side in (0, 1):
            halo = left_ref if side == 0 else right_ref
            for d in range(half, 0, -1):
                k = half - d if side == 0 else half + d
                n = STEP * d
                shift = STEP * (k - half)
                low = 0 if side == 0 else own - n
                source = reach - n if side == 0 else 0
                near = info_ref[1 + k][:, reach + low : reach + low + n] == 1
                matched = near & (
                    ids[:, reach + low + shift : reach + low + shift + n]
                    == ids[:, reach + low : reach + low + n]
                )
                columns = mask_columns(matched)
                lhs = jnp.concatenate(
                    [
                        halo[r, source : source + n, :] * spread(columns[:, r : r + 1], features)
                        for r in range(rows)
                    ],
                    axis=0,
                )
                product = dot(lhs, conv_w_ref[k], 1, 0).reshape(rows, n, features)
                if d == half:
                    halo_acc[:, low : low + n, :] = product
                else:
                    halo_acc[:, low : low + n, :] += product

    conv_bias = vec_ref[0:1, :]
    gain_one = vec_ref[1:2, :]
    bias_one = vec_ref[2:3, :]
    gain_two = vec_ref[3:4, :]
    bias_two = vec_ref[4:5, :]
    at = pl.ds(step * block_rows, block_rows)
    span = pl.ds(step * size, size)
    conv = (acc_ref[...] + halo_acc[at, :, :]).reshape(size, features)
    hidden = (conv + conv_bias).astype(BF)
    hidden_ref[...] = hidden.reshape(hidden_ref.shape)
    hid = hidden.astype(F32)
    act = hid * (0.5 + 0.5 * lax.erf(hid * RSQRT2))
    centered = act - jnp.mean(act, axis=1, keepdims=True)
    scale = lax.rsqrt(jnp.mean(centered * centered, axis=1, keepdims=True) + EPS)
    mixed = x_ref[...].reshape(size, features).astype(F32) + (
        centered * scale * gain_one + bias_one
    )
    mixed_low = mixed.astype(BF)
    low_ref[...] = mixed_low.reshape(low_ref.shape)
    chunk = 512
    projected = None
    for j in range(hidden_units // chunk):
        cols = slice(j * chunk, (j + 1) * chunk)
        up = dot(mixed_low, w_in_ref[:, cols], 1, 0) + b_in_ref[:, cols]
        cdf, bell = cdf_and_exp(up)
        act_low = (up * cdf).astype(BF)
        slope_ref[:, cols] = (cdf + up * bell * RSQRT2PI).astype(BF)
        act_scr[span, cols] = act_low
        part = dot(act_low, w_out_ref[cols, :], 1, 0)
        projected = part if projected is None else projected + part
    centered = projected - jnp.mean(projected, axis=1, keepdims=True)
    scale = lax.rsqrt(jnp.mean(centered * centered, axis=1, keepdims=True) + EPS)
    xhat = centered * scale
    out_ref[...] = (mixed + (xhat * gain_two + bias_two)).astype(BF).reshape(out_ref.shape)
    ct = ct_ref[...].reshape(size, features).astype(F32)
    ct_xhat = ct * xhat
    gain_ref[...] += fold(ct_xhat)
    bias_ref[...] += fold(ct)
    e = ct * gain_two
    mean_e = jnp.mean(e, axis=1, keepdims=True)
    mean_ex = jnp.mean(e * xhat, axis=1, keepdims=True)
    gproj = (scale * (e - mean_e - xhat * mean_ex)).astype(BF)
    gproj_ref[...] = gproj
    gp_scr[span, :] = gproj

    @pl.when(step == steps - 1)
    def _():
        n_wide, n_narrow = blocks
        height, width = hidden_units // n_narrow, features // n_wide
        for n in range(n_narrow):
            product = dot(act_scr[:, n * height : (n + 1) * height], gp_scr[...], 0, 0).astype(BF)
            for w in range(n_wide):
                place_block(
                    gw_ref, product[:, w * width : (w + 1) * width], w, n, slice(0, height), blocks
                )
        if blocks != (1, 1):
            ship(gw_ref, keep_ref, send_ref, sems)


def gradient_outputs(blocks, height, width):
    if blocks == (1, 1):
        dims = (1, 1, height, width)
        return [shape(dims, BF)], [whole(dims)], []
    n_wide, n_narrow = blocks
    dims = (n_wide * n_narrow // 2, height // n_narrow, width // n_wide)
    return (
        [shape(dims, BF)] * 2,
        [pl.BlockSpec(memory_space=pl.ANY)] * 2,
        [pltpu.VMEM((2,) + dims, BF), pltpu.SemaphoreType.DMA((2,))],
    )


def forward(blocks, info, acc, left, right, x, ct, conv_w, w_in, w_out, vec, b_in):
    rows, own, features = x.shape
    hidden_units = w_in.shape[1]
    block_rows = 2
    steps = rows // block_rows
    size = block_rows * own
    total = rows * own
    row_block = pl.BlockSpec((block_rows, own, features), lambda i: (i, 0, 0))
    shapes, specs, scratch = gradient_outputs(blocks, hidden_units, features)
    return pl.pallas_call(
        functools.partial(forward_kernel, blocks),
        grid=(steps,),
        in_specs=[
            whole(info.shape), row_block, whole(left.shape), whole(right.shape), row_block,
            row_block, whole(conv_w.shape), whole(w_in.shape), whole(w_out.shape),
            whole(vec.shape), whole(b_in.shape),
        ],
        out_specs=[
            row_block, row_block, row_block,
            pl.BlockSpec((size, features), lambda i: (i, 0)),
            pl.BlockSpec((size, hidden_units), lambda i: (i, 0)),
            whole((8, features)), whole((8, features)),
        ] + specs,
        out_shape=[
            shape(x.shape, BF), shape(x.shape, BF), shape(x.shape, BF),
            shape((total, features), BF), shape((total, hidden_units), BF),
            shape((8, features), F32), shape((8, features), F32),
        ] + shapes,
        scratch_shapes=[
            pltpu.VMEM(x.shape, F32), pltpu.VMEM((total, hidden_units), BF),
            pltpu.VMEM((total, features), BF),
        ] + scratch,
        compiler_params=params(),
        cost_estimate=cost(2 * total * features * (3 * hidden_units + 2.5 * features), 40e6),
        name="forward",
    )(info, acc, left, right, x, ct, conv_w, w_in, w_out, vec, b_in)


def backward_kernel(
    blocks,
    gproj_ref, slope_ref, low_ref, hidden_ref, ct_ref, w_in_ref, w_out_ref, vec_ref,
    gmixed_ref, gh_ref, b_in_ref, gain_ref, bias_ref, conv_b_ref, *rest,
):
    if blocks == (1, 1):
        gw_ref, up_scr, low_scr = rest
    else:
        keep_ref, send_ref, up_scr, low_scr, gw_ref, sems = rest
    step = pl.program_id(0)
    steps = pl.num_programs(0)
    size = gproj_ref.shape[0]
    features = low_ref.shape[-1]
    hidden_units = w_in_ref.shape[1]

    @pl.when(step == 0)
    def _():
        for ref in (b_in_ref, gain_ref, bias_ref, conv_b_ref):
            ref[...] = jnp.zeros_like(ref)

    span = pl.ds(step * size, size)
    gain_one = vec_ref[1:2, :]
    gproj = gproj_ref[...]
    chunk = 512
    total = None
    for j in range(hidden_units // chunk):
        cols = slice(j * chunk, (j + 1) * chunk)
        g_act = dot(gproj, w_out_ref[cols, :], 1, 1)
        up_low = (g_act * slope_ref[:, cols].astype(F32)).astype(BF)
        up_scr[span, cols] = up_low
        b_in_ref[:, cols] += fold(up_low.astype(F32))
        part = dot(up_low, w_in_ref[:, cols], 1, 1)
        total = part if total is None else total + part
    mixed_low = low_ref[...].reshape(size, features)
    low_scr[span, :] = mixed_low
    g_mixed = ct_ref[...].reshape(size, features).astype(F32) + total
    gmixed_ref[...] = g_mixed.reshape(gmixed_ref.shape)
    hid = hidden_ref[...].reshape(size, features).astype(F32)
    cdf, bell = cdf_and_exp(hid)
    act = hid * cdf
    centered = act - jnp.mean(act, axis=1, keepdims=True)
    scale = lax.rsqrt(jnp.mean(centered * centered, axis=1, keepdims=True) + EPS)
    yhat = centered * scale
    gain_ref[...] += fold(g_mixed * yhat)
    bias_ref[...] += fold(g_mixed)
    e = g_mixed * gain_one
    mean_e = jnp.mean(e, axis=1, keepdims=True)
    mean_ey = jnp.mean(e * yhat, axis=1, keepdims=True)
    g_hidden = scale * (e - mean_e - yhat * mean_ey) * (cdf + hid * bell * RSQRT2PI)
    g_low = g_hidden.astype(BF)
    gh_ref[...] = g_low.reshape(gh_ref.shape)
    conv_b_ref[...] += fold(g_low.astype(F32))

    @pl.when(step == steps - 1)
    def _():
        n_wide, n_narrow = blocks
        height, width = features // n_narrow, hidden_units // n_wide
        for w in range(n_wide):
            product = dot(low_scr[...], up_scr[:, w * width : (w + 1) * width], 0, 0).astype(BF)
            for n in range(n_narrow):
                place_block(
                    gw_ref, product[n * height : (n + 1) * height, :], w, n, slice(0, height), blocks
                )
        if blocks != (1, 1):
            ship(gw_ref, keep_ref, send_ref, sems)


def backward(blocks, gproj, slope, mixed_low, hidden, ct, w_in, w_out, vec):
    rows, own, features = hidden.shape
    hidden_units = w_in.shape[1]
    block_rows = 2
    steps = rows // block_rows
    size = block_rows * own
    total = rows * own
    row_block = pl.BlockSpec((block_rows, own, features), lambda i: (i, 0, 0))
    shapes, specs, scratch = gradient_outputs(blocks, features, hidden_units)
    return pl.pallas_call(
        functools.partial(backward_kernel, blocks),
        grid=(steps,),
        in_specs=[
            pl.BlockSpec((size, features), lambda i: (i, 0)),
            pl.BlockSpec((size, hidden_units), lambda i: (i, 0)),
            row_block, row_block, row_block, whole(w_in.shape), whole(w_out.shape),
            whole(vec.shape),
        ],
        out_specs=[
            row_block, row_block, whole((8, hidden_units)), whole((8, features)),
            whole((8, features)), whole((8, features)),
        ] + specs,
        out_shape=[
            shape(hidden.shape, F32), shape(hidden.shape, BF), shape((8, hidden_units), F32),
            shape((8, features), F32), shape((8, features), F32), shape((8, features), F32),
        ] + shapes,
        scratch_shapes=[
            pltpu.VMEM((total, hidden_units), BF), pltpu.VMEM((total, features), BF),
        ] + scratch,
        compiler_params=params(),
        cost_estimate=cost(2 * total * features * 3 * hidden_units, 30e6),
        name="backward",
    )(gproj, slope, mixed_low, hidden, ct, w_in, w_out, vec)


def weight_kernel(blocks, info_ref, x_ref, left_ref, right_ref, gh_ref, *rest):
    if blocks == (1, 1):
        gw_ref, ext = rest
    else:
        keep_ref, send_ref, ext, gw_ref, sems = rest
    tap = pl.program_id(0)
    taps = pl.num_programs(0)
    rows, own, features = x_ref.shape
    reach = left_ref.shape[1]

    @pl.when(tap == 0)
    def _():
        ext[:, 0:reach, :] = left_ref[...]
        ext[:, reach : reach + own, :] = x_ref[...]
        ext[:, reach + own : own + 2 * reach, :] = right_ref[...]

    ids = info_ref[0]
    whole_row = own + 2 * reach
    moved = pltpu.roll(ids, whole_row - STEP * tap, 1)[:, :own]
    matched = (moved == ids[:, reach : reach + own]) & (
        info_ref[1 + tap][:, reach : reach + own] == 1
    )
    columns = mask_columns(matched)
    at = pl.ds(pl.multiple_of(STEP * tap, STEP), own)
    lhs = jnp.concatenate(
        [ext[r, at, :] * spread(columns[:, r : r + 1], features) for r in range(rows)], axis=0
    )
    product = dot(lhs, gh_ref[...].reshape(rows * own, features), 0, 0).astype(BF)
    n_wide, n_narrow = blocks
    height, width = features // n_narrow, features // n_wide
    rows_at = pl.ds(pl.multiple_of(tap * height, height), height)
    for n in range(n_narrow):
        for w in range(n_wide):
            place_block(
                gw_ref,
                product[n * height : (n + 1) * height, w * width : (w + 1) * width],
                w, n, rows_at, blocks,
            )

    if blocks != (1, 1):

        @pl.when(tap == taps - 1)
        def _():
            ship(gw_ref, keep_ref, send_ref, sems)


def weight_gradient(blocks, info, x, left, right, gh, taps):
    rows, own, features = x.shape
    reach = left.shape[1]
    shapes, specs, scratch = gradient_outputs(blocks, taps * features, features)
    return pl.pallas_call(
        functools.partial(weight_kernel, blocks),
        grid=(taps,),
        in_specs=[whole(v.shape) for v in (info, x, left, right, gh)],
        out_specs=specs,
        out_shape=shapes,
        scratch_shapes=[pltpu.VMEM((rows, own + 2 * reach, features), BF)] + scratch,
        compiler_params=params(),
        cost_estimate=cost(2 * rows * own * features * features * taps, 12e6),
        name="weight_gradient",
    )(info, x, left, right, gh)


def input_kernel(info_ref, gmixed_ref, gh_ref, left_ref, right_ref, wt_ref, gx_ref, patches):
    block_rows, own, features = gh_ref.shape
    reach = left_ref.shape[1]
    taps = info_ref.shape[1] - 1
    for r in range(block_rows):
        ids = info_ref[r, 0:1, :]
        matched = []
        for k in range(taps):
            start = STEP * (taps - 1 - k)
            same = (ids[:, start : start + own] == ids[:, reach : reach + own]) & (
                info_ref[r, 1 + k : 2 + k, start : start + own] == 1
            )
            matched.append(jnp.where(same, 1.0, 0.0).astype(F32))
        matched.append(jnp.zeros((16 - taps, own), F32))
        columns = jnp.concatenate(matched, axis=0).T
        for k in range(taps):
            start = STEP * (taps - 1 - k)
            mask = spread(columns[:, k : k + 1], features)
            cols = slice(k * features, (k + 1) * features)
            base = r * own
            if start < reach:
                n = reach - start
                patches[base : base + n, cols] = left_ref[r, start:reach, :] * mask[:n]
                patches[base + n : base + own, cols] = gh_ref[r, : own - n, :] * mask[n:]
            elif start == reach:
                patches[base : base + own, cols] = gh_ref[r] * mask
            else:
                n = own - (start - reach)
                patches[base : base + n, cols] = gh_ref[r, start - reach :, :] * mask[:n]
                patches[base + n : base + own, cols] = right_ref[r, : own - n, :] * mask[n:]
    g_in = dot(patches[...], wt_ref[...], 1, 0).astype(BF).astype(F32)
    gx_ref[...] = gmixed_ref[...] + g_in.reshape(gx_ref.shape)


def input_gradient(info, gmixed, gh, left, right, wt):
    rows, own, features = gh.shape
    reach = left.shape[1]
    block_rows = 2
    row_block = pl.BlockSpec((block_rows, own, features), lambda i: (i, 0, 0))
    halo_block = pl.BlockSpec((block_rows, reach, features), lambda i: (i, 0, 0))
    return pl.pallas_call(
        input_kernel,
        grid=(rows // block_rows,),
        in_specs=[
            pl.BlockSpec((block_rows,) + info.shape[1:], lambda i: (i, 0, 0)),
            row_block, row_block, halo_block, halo_block, whole(wt.shape),
        ],
        out_specs=row_block,
        out_shape=shape(gh.shape, F32),
        scratch_shapes=[pltpu.VMEM((block_rows * own, wt.shape[0]), BF)],
        compiler_params=params(),
        cost_estimate=cost(2 * rows * own * wt.shape[0] * features, 18e6),
        name="input_gradient",
    )(info, gmixed, gh, left, right, wt)


def flip(value, axis, bit):
    size = lax.axis_size(axis)
    return lax.ppermute(value, axis, [(i, i ^ bit) for i in range(size)])


def add(a, b):
    return a.astype(F32) + b.astype(F32)


def after_core_kernel(keep, got, a_keep, a_send, b_keep, b_send):
    rows = keep.shape[1] // 2
    for y in range(2):
        for x in range(2):
            src = slice(8 * y + 4 * x, 8 * y + 4 * x + 4)
            top = add(keep[src, :rows, :], got[src, :rows, :]).astype(BF)
            (a_send if x else a_keep)[4 * y : 4 * y + 4] = top
            bottom = add(keep[src, rows:, :], got[src, rows:, :]).astype(BF)
            (b_send if y else b_keep)[4 * x : 4 * x + 4] = bottom


def after_first_kernel(a_keep, a_got, b_keep, b_got, a_next, a_send, b_next, b_send):
    for keep, got, stay, send in ((a_keep, a_got, a_next, a_send), (b_keep, b_got, b_next, b_send)):
        stay[...] = add(keep[:4], got[:4]).astype(BF)
        send[...] = add(keep[4:], got[4:]).astype(BF)


def after_second_kernel(a_keep, a_got, b_keep, b_got, z0, z1, z2, z3):
    rows = a_keep.shape[1]
    for i, ref in enumerate((z0, z1, z2, z3)):
        ref[:rows, :] = add(a_keep[i], a_got[i]).astype(BF)
        ref[rows:, :] = add(b_keep[i], b_got[i]).astype(BF)


def last_kernel(z0, z1, z2, z3, out):
    out[...] = add(z0[...], z1[...]) + add(z2[...], z3[...])


def small(kernel, operands, dims, dtype=BF):
    moved = sum(v.size * v.dtype.itemsize for v in operands) * 2
    return pl.pallas_call(
        kernel,
        out_shape=[shape(d, dtype) for d in dims],
        compiler_params=params(),
        cost_estimate=cost(moved / 2, moved),
        name=kernel.__name__,
    )(*operands)


def scatter_sum(keep, send):
    _, rows, width = keep.shape
    got = flip(send, "wide", 1)
    half = (8, rows // 2, width)
    a_keep, a_send, b_keep, b_send = small(after_core_kernel, (keep, got), [half] * 4)
    a_got, b_got = flip(a_send, "narrow", 1), flip(b_send, "wide", 2)
    quarter = (4, rows // 2, width)
    a_keep, a_send, b_keep, b_send = small(
        after_first_kernel, (a_keep, a_got, b_keep, b_got), [quarter] * 4
    )
    a_got, b_got = flip(a_send, "wide", 2), flip(b_send, "narrow", 1)
    z = small(after_second_kernel, (a_keep, a_got, b_keep, b_got), [(rows, width)] * 4)
    others = [flip(z[i], "narrow", 2 * i) for i in (1, 2, 3)]
    return small(last_kernel, (z[0], *others), [(rows, width)], F32)[0]


def body(
    inputs, conv_w, conv_b, ln1_gain, ln1_bias, w_in, b_in, w_out, ln2_gain, ln2_bias,
    segments, tap_mask, cotangent,
):
    rows, own, features = inputs.shape
    taps = conv_w.shape[0]
    reach = STEP * (taps // 2)
    hidden_units = w_in.shape[1]
    n_wide, n_narrow = lax.axis_size("wide"), lax.axis_size("narrow")
    by_hand = (n_wide, n_narrow) == (4, 8)
    blocks = (4, 8) if by_hand else (1, 1)

    to_right = [(i, i + 1) for i in range(n_wide - 1)]
    to_left = [(i + 1, i) for i in range(n_wide - 1)]

    def halos(value, dim):
        last = value.shape[dim]
        left = lax.ppermute(lax.slice_in_dim(value, last - reach, last, axis=dim), "wide", to_right)
        right = lax.ppermute(lax.slice_in_dim(value, 0, reach, axis=dim), "wide", to_left)
        return left, right

    info = jnp.concatenate([segments[None] + 1, jnp.transpose(tap_mask, (1, 0, 2))], axis=0)
    info_left, info_right = halos(info, 2)
    x_left, x_right = halos(inputs, 1)
    info_ext = jnp.concatenate([info_left, info, info_right], axis=2)
    info_rows = jnp.transpose(info_ext, (1, 0, 2))
    vec = jnp.stack([conv_b, ln1_gain, ln1_bias, ln2_gain, ln2_bias]).astype(F32)
    vec = jnp.pad(vec, ((0, 3), (0, 0)))
    wt = jnp.transpose(conv_w, (0, 2, 1)).reshape(taps * features, features)

    acc = conv_inner(info, inputs, conv_w)
    out, mixed_low, hidden, gproj, slope, gain_two, bias_two, *gw_out = forward(
        blocks, info_ext, acc, x_left, x_right, inputs, cotangent, conv_w, w_in, w_out, vec,
        b_in.astype(F32)[None],
    )
    gmixed, gh, gb_in, gain_one, bias_one, gconv_b, *gw_in = backward(
        blocks, gproj, slope, mixed_low, hidden, cotangent, w_in, w_out, vec
    )
    gh_left, gh_right = halos(gh, 1)
    gconv = weight_gradient(blocks, info_ext, inputs, x_left, x_right, gh, taps)
    grad_inputs = input_gradient(info_rows, gmixed, gh, gh_left, gh_right, wt)

    if by_hand:
        grad_w_out = scatter_sum(*gw_out)
        grad_w_in = scatter_sum(*gw_in)
        grad_conv = scatter_sum(*gconv).reshape(taps, features // n_narrow, features // n_wide)
    else:

        def reduce(value, dims, wide_dim, narrow_dim):
            value = lax.psum_scatter(
                value.reshape(dims), "narrow", scatter_dimension=narrow_dim, tiled=True
            )
            return lax.psum_scatter(value, "wide", scatter_dimension=wide_dim, tiled=True).astype(
                F32
            )

        grad_w_out = reduce(gw_out[0], (hidden_units, features), 1, 0)
        grad_w_in = reduce(gw_in[0], (features, hidden_units), 1, 0)
        grad_conv = reduce(gconv[0], (taps, features, features), 2, 1)
    sums = jnp.concatenate(
        [v.sum(0) for v in (gconv_b, gain_one, bias_one, gb_in, gain_two, bias_two)]
    )
    sums = lax.psum(sums, ("wide", "narrow"))
    cuts = [features, 2 * features, 3 * features]
    cuts += [cuts[-1] + hidden_units, cuts[-1] + hidden_units + features]
    vectors = jnp.split(sums, cuts)
    return (
        out, grad_inputs, grad_conv, vectors[0], vectors[1], vectors[2], grad_w_in, vectors[3],
        grad_w_out, vectors[4], vectors[5],
    )


def solution(mesh):
    split = P("narrow", "wide", None)
    placed = (split,) + (P(),) * 9 + (P("narrow", "wide"), P("narrow", None, "wide"), split)
    return jax.shard_map(
        body,
        mesh=mesh,
        in_specs=placed,
        out_specs=(
            split, split, P(None, "narrow", "wide"), P(), P(), P(), P("narrow", "wide"), P(),
            P("narrow", "wide"), P(), P(),
        ),
        check_vma=False,
    )
```

```python
import functools
from typing import Any, NamedTuple

import jax
import jax.numpy as jnp
from jax import lax
from jax.experimental import pallas as pl
from jax.experimental.pallas import tpu as pltpu
from jax.sharding import PartitionSpec as P

STEP = 32
BF = jnp.bfloat16
F32 = jnp.float32
RSQRT2 = 0.7071067811865476
RSQRT2PI = 0.3989422804014327
EPS = 1e-05


def params(mebibytes):
    return pltpu.CompilerParams(vmem_limit_bytes=mebibytes * 1024 * 1024)


def cost(flops, moved, transcendentals=0):
    return pl.CostEstimate(
        flops=int(flops), bytes_accessed=int(moved), transcendentals=int(transcendentals)
    )


def whole(shape):
    rank = len(shape)
    return pl.BlockSpec(shape, lambda *_: (0,) * rank, pipeline_mode=pl.Buffered(1))


def shape(dims, dtype):
    return jax.ShapeDtypeStruct(dims, dtype)


def mask_columns(matched):
    return jnp.where(matched, 1.0, 0.0).astype(F32).T


def spread(column, width):
    wide = jnp.broadcast_to(column, (column.shape[0], 128)).astype(BF)
    return jnp.concatenate([wide] * (width // 128), axis=1)


def dot(left, right, left_dim, right_dim):
    return lax.dot_general(
        left, right, (((left_dim,), (right_dim,)), ((), ())), preferred_element_type=F32
    )


def cdf_and_exp(values):
    return 0.5 + 0.5 * lax.erf(values * RSQRT2), jnp.exp(-0.5 * values * values)


def fold(values):
    return values.reshape(-1, 8, values.shape[-1]).sum(0)


def put_masked(lhs, sources, columns, n, features):
    for r, source in enumerate(sources):
        lhs[r * n : (r + 1) * n, :] = source * spread(columns[:, r : r + 1], features)


def conv_inner_kernel(info_ref, x_ref, w_ref, acc_ref, even, odd):
    step = pl.program_id(0)
    rows, own, features = x_ref.shape
    taps = info_ref.shape[0] - 1
    half = taps // 2
    order = [half] + [k for k in range(taps) if k != half]
    buffers = (even, odd)

    def span(k):
        shift = STEP * (k - half)
        return max(0, -shift), own - max(0, shift), shift

    def build(i):
        k = order[i]
        low, high, shift = span(k)
        ids = info_ref[0]
        matched = (ids[:, low + shift : high + shift] == ids[:, low:high]) & (
            info_ref[1 + k][:, low:high] == 1
        )
        put_masked(
            buffers[i % 2],
            [x_ref[r, low + shift : high + shift, :] for r in range(rows)],
            mask_columns(matched), high - low, features,
        )

    def run(i):
        low, high, _ = span(order[i])
        n = high - low
        if i + 1 < taps:
            build(i + 1)
        product = dot(buffers[i % 2][: rows * n, :], w_ref[0], 1, 0).reshape(rows, n, features)
        if i == 0:
            acc_ref[...] = product
        else:
            acc_ref[:, low:high, :] += product

    pl.when(step == 0)(functools.partial(build, 0))
    for i in range(taps):
        pl.when(step == i)(functools.partial(run, i))


def conv_inner(info, x, conv_w):
    rows, own, features = x.shape
    taps = conv_w.shape[0]
    half = taps // 2

    def tap_of(i):
        return jnp.where(i == 0, half, jnp.where(i <= half, i - 1, i))

    return pl.pallas_call(
        conv_inner_kernel,
        grid=(taps,),
        in_specs=[
            whole(info.shape),
            whole(x.shape),
            pl.BlockSpec((1, features, features), lambda i: (tap_of(i), 0, 0)),
        ],
        out_specs=whole(x.shape),
        out_shape=shape(x.shape, F32),
        scratch_shapes=[pltpu.VMEM((rows * own, features), BF)] * 2,
        compiler_params=params(20),
        cost_estimate=cost(2 * rows * own * features * features * taps * 0.72, 11e6),
        name="conv_inner",
    )(info, x, conv_w)


def conv_outer_kernel(info_ref, left_ref, right_ref, w_ref, vec_ref, acc_hbm, hidden_ref, acc, even, odd, sem):
    step = pl.program_id(0)
    rows, own, features = hidden_ref.shape
    taps = info_ref.shape[0] - 1
    half = taps // 2
    reach = STEP * half
    order = [k for k in range(taps) if k != half]
    buffers = (even, odd)
    load = pltpu.make_async_copy(acc_hbm, acc, sem)

    def span(k):
        n = STEP * abs(k - half)
        return (0 if k < half else own - n), n

    def build(i):
        k = order[i]
        low, n = span(k)
        left = k < half
        source = reach - n if left else 0
        shift = -n if left else n
        at = reach + low
        ids = info_ref[0]
        matched = (info_ref[1 + k][:, at : at + n] == 1) & (
            ids[:, at + shift : at + shift + n] == ids[:, at : at + n]
        )
        halo = left_ref if left else right_ref
        put_masked(
            buffers[i % 2], [halo[r, source : source + n, :] for r in range(rows)],
            mask_columns(matched), n, features,
        )

    def run(i):
        low, n = span(order[i])
        if i + 1 < len(order):
            build(i + 1)
        product = dot(buffers[i % 2][: rows * n, :], w_ref[0], 1, 0).reshape(rows, n, features)
        acc[:, low : low + n, :] += product

    @pl.when(step == 0)
    def _():
        load.start()
        build(0)
        load.wait()

    for i in range(len(order)):
        pl.when(step == i)(functools.partial(run, i))

    @pl.when(step == len(order) - 1)
    def _():
        hidden_ref[...] = (acc[...] + vec_ref[0:1, :]).astype(BF)


def conv_outer(info, acc, left, right, conv_w, vec):
    rows, own, features = acc.shape
    reach = left.shape[1]
    taps = conv_w.shape[0]
    half = taps // 2
    return pl.pallas_call(
        conv_outer_kernel,
        grid=(taps - 1,),
        in_specs=[
            whole(info.shape),
            whole(left.shape),
            whole(right.shape),
            pl.BlockSpec((1, features, features), lambda i: (jnp.where(i < half, i, i + 1), 0, 0)),
            whole(vec.shape),
            pl.BlockSpec(memory_space=pl.ANY),
        ],
        out_specs=whole(acc.shape),
        out_shape=shape(acc.shape, BF),
        scratch_shapes=[pltpu.VMEM(acc.shape, F32)]
        + [pltpu.VMEM((rows * reach, features), BF)] * 2
        + [pltpu.SemaphoreType.DMA],
        compiler_params=params(18),
        cost_estimate=cost(2 * rows * own * features * features * taps * 0.28, 11e6),
        name="conv_outer",
    )(info, left, right, conv_w, vec, acc)


def place_block(out_ref, value, dest_wide, dest_narrow, rows_at, blocks):
    if blocks == (1, 1):
        out_ref[0, 0, rows_at, :] = value
        return
    rel_wide = lax.axis_index("wide") ^ dest_wide
    rel_narrow = lax.axis_index("narrow") ^ dest_narrow
    index = (rel_wide >> 1) * 8 + (rel_narrow & 1) * 4 + (rel_narrow >> 1)
    out_ref[rel_wide & 1, index, rows_at, :] = value


def ship(pairs, sems):
    copies = [pltpu.make_async_copy(src, dst, sems.at[i]) for i, (src, dst) in enumerate(pairs)]
    for copy in copies:
        copy.start()
    for copy in copies:
        copy.wait()


def gradient_outputs(blocks, height, width, lanes=None):
    if blocks == (1, 1):
        dims = (1, 1, height, width)
        return [shape(dims, BF)], [whole(dims)], []
    n_wide, n_narrow = blocks
    height, width = height // n_narrow, width // n_wide
    if lanes is not None:
        height, width = height * width // lanes, lanes
    dims = (n_wide * n_narrow // 2, height, width)
    return (
        [shape(dims, BF)] * 2,
        [pl.BlockSpec(memory_space=pl.ANY)] * 2,
        [pltpu.VMEM((2,) + dims, BF), pltpu.SemaphoreType.DMA((2,))],
    )


def moments(values):
    centered = values - jnp.mean(values, axis=1, keepdims=True)
    return centered, lax.rsqrt(jnp.mean(centered * centered, axis=1, keepdims=True) + EPS)


def middle_kernel(
    blocks,
    hidden_ref, x_ref, ct_ref, w_in_ref, w_out_ref, vec_ref, b_in_ref,
    out_ref, gmixed_ref, gh_ref, sums_ref, *rest,
):
    if blocks == (1, 1):
        gw_out_ref, gw_in_ref, *rest = rest
    else:
        (keep_out, send_out, keep_in, send_in, *rest) = rest
    (
        act_scr, slope_scr, up_scr, gp_scr, gw_out_acc, gw_in_acc, b_in_acc, gain_one_acc,
        bias_one_acc, gain_two_acc, bias_two_acc, conv_b_acc, *rest,
    ) = rest
    if blocks != (1, 1):
        gw_out_ref, gw_in_ref, sems = rest
    step = pl.program_id(0)
    steps = pl.num_programs(0)
    size = act_scr.shape[0]
    features, hidden_units = w_in_ref.shape

    @pl.when(step == 0)
    def _():
        for ref in (
            act_scr, gp_scr, gw_out_acc, gw_in_acc, b_in_acc, gain_one_acc, bias_one_acc,
            gain_two_acc, bias_two_acc, conv_b_acc,
        ):
            ref[...] = jnp.zeros_like(ref)

    gain_one = vec_ref[1:2, :]
    bias_one = vec_ref[2:3, :]
    gain_two = vec_ref[3:4, :]
    bias_two = vec_ref[4:5, :]
    chunk = 512
    count = hidden_units // chunk
    pieces = [slice(j * chunk, (j + 1) * chunk) for j in range(count)]

    def out_part(cols):
        gw_out_acc[cols, :] += dot(act_scr[:, cols], gp_scr[...], 0, 0)

    for cols in pieces:
        out_part(cols)
    hid = hidden_ref[...].reshape(size, features).astype(F32)
    centered, scale = moments(hid * (0.5 + 0.5 * lax.erf(hid * RSQRT2)))
    mixed = x_ref[...].reshape(size, features).astype(F32) + (
        centered * scale * gain_one + bias_one
    )
    mixed_low = mixed.astype(BF)

    def up_part(cols):
        return dot(mixed_low, w_in_ref[:, cols], 1, 0) + b_in_ref[:, cols]

    projected = None
    up = up_part(pieces[0])
    for j, cols in enumerate(pieces):
        ahead = up_part(pieces[j + 1]) if j + 1 < count else None
        cdf, bell = cdf_and_exp(up)
        act_low = (up * cdf).astype(BF)
        slope_scr[:, cols] = cdf + up * bell * RSQRT2PI
        act_scr[:, cols] = act_low
        part = dot(act_low, w_out_ref[cols, :], 1, 0)
        projected = part if projected is None else projected + part
        up = ahead
    centered, scale = moments(projected)
    xhat = centered * scale
    out_ref[...] = (mixed + (xhat * gain_two + bias_two)).astype(BF).reshape(out_ref.shape)
    ct = ct_ref[...].reshape(size, features).astype(F32)
    gain_two_acc[...] += fold(ct * xhat)
    bias_two_acc[...] += fold(ct)
    e = ct * gain_two
    mean_e = jnp.mean(e, axis=1, keepdims=True)
    mean_ex = jnp.mean(e * xhat, axis=1, keepdims=True)
    gproj = (scale * (e - mean_e - xhat * mean_ex)).astype(BF)
    gp_scr[...] = gproj

    for cols in pieces:
        g_act = dot(gproj, w_out_ref[cols, :], 1, 1)
        up_low = (g_act * slope_scr[:, cols]).astype(BF)
        up_scr[:, cols] = up_low
        b_in_acc[:, cols] += fold(up_low.astype(F32))
    total = dot(up_scr[...], w_in_ref[...], 1, 1)
    for cols in pieces:
        gw_in_acc[:, cols] += dot(mixed_low, up_scr[:, cols], 0, 0)
    g_mixed = ct_ref[...].reshape(size, features).astype(F32) + total
    gmixed_ref[...] = g_mixed.reshape(gmixed_ref.shape)
    hid = hidden_ref[...].reshape(size, features).astype(F32)
    cdf, bell = cdf_and_exp(hid)
    centered, scale = moments(hid * cdf)
    yhat = centered * scale
    gain_one_acc[...] += fold(g_mixed * yhat)
    bias_one_acc[...] += fold(g_mixed)
    e = g_mixed * gain_one
    mean_e = jnp.mean(e, axis=1, keepdims=True)
    mean_ey = jnp.mean(e * yhat, axis=1, keepdims=True)
    g_hidden = scale * (e - mean_e - yhat * mean_ey) * (cdf + hid * bell * RSQRT2PI)
    g_low = g_hidden.astype(BF)
    gh_ref[...] = g_low.reshape(gh_ref.shape)
    conv_b_acc[...] += fold(g_low.astype(F32))

    @pl.when(step == steps - 1)
    def _():
        for cols in pieces:
            out_part(cols)
        row = 0
        for ref in (conv_b_acc, gain_one_acc, bias_one_acc, b_in_acc, gain_two_acc, bias_two_acc):
            summed = jnp.sum(ref[...], axis=0, keepdims=True)
            for j in range(ref.shape[1] // 128):
                sums_ref[row : row + 1, :] = summed[:, j * 128 : (j + 1) * 128]
                row += 1
        sums_ref[row:, :] = jnp.zeros_like(sums_ref[row:, :])
        n_wide, n_narrow = blocks
        height, width = features // n_narrow, hidden_units // n_wide
        lanes = gw_in_ref.shape[-1]
        for w in range(n_wide):
            product = gw_in_acc[:, w * width : (w + 1) * width].astype(BF)
            for n in range(n_narrow):
                for j in range(width // lanes):
                    place_block(
                        gw_in_ref,
                        product[n * height : (n + 1) * height, j * lanes : (j + 1) * lanes],
                        w, n, slice(j * height, (j + 1) * height), blocks,
                    )
        height, width = hidden_units // n_narrow, features // n_wide
        for n in range(n_narrow):
            product = gw_out_acc[n * height : (n + 1) * height, :].astype(BF)
            for w in range(n_wide):
                place_block(
                    gw_out_ref, product[:, w * width : (w + 1) * width], w, n, slice(0, height),
                    blocks,
                )
        if blocks != (1, 1):
            ship(
                (
                    (gw_in_ref.at[0], keep_in), (gw_in_ref.at[1], send_in),
                    (gw_out_ref.at[0], keep_out), (gw_out_ref.at[1], send_out),
                ),
                sems,
            )


def middle(blocks, hidden, x, ct, w_in, w_out, vec, b_in):
    rows, own, features = x.shape
    hidden_units = w_in.shape[1]
    block_rows = 2
    size = block_rows * own
    total = rows * own
    row_block = pl.BlockSpec((block_rows, own, features), lambda i: (i, 0, 0))
    out_shapes, out_specs, out_scratch = gradient_outputs(blocks, hidden_units, features)
    in_shapes, in_specs, in_scratch = gradient_outputs(blocks, features, hidden_units, 128)
    sums = ((5 * features + hidden_units) // 128 + 63) // 64 * 64
    sems = [] if blocks == (1, 1) else [pltpu.SemaphoreType.DMA((4,))]
    narrow = pltpu.VMEM((8, features), F32)
    return pl.pallas_call(
        functools.partial(middle_kernel, blocks),
        grid=(rows // block_rows,),
        in_specs=[
            row_block, row_block, row_block, whole(w_in.shape), whole(w_out.shape),
            whole(vec.shape), whole(b_in.shape),
        ],
        out_specs=[row_block, row_block, row_block, whole((sums, 128))] + out_specs + in_specs,
        out_shape=[
            shape(x.shape, BF), shape(x.shape, F32), shape(x.shape, BF), shape((sums, 128), F32),
        ] + out_shapes + in_shapes,
        scratch_shapes=[
            pltpu.VMEM((size, hidden_units), BF), pltpu.VMEM((size, hidden_units), F32),
            pltpu.VMEM((size, hidden_units), BF), pltpu.VMEM((size, features), BF),
            pltpu.VMEM((hidden_units, features), F32), pltpu.VMEM((features, hidden_units), F32),
            pltpu.VMEM((8, hidden_units), F32), narrow, narrow, narrow, narrow, narrow,
        ] + out_scratch[:1] + in_scratch[:1] + sems,
        compiler_params=params(46),
        cost_estimate=cost(2 * total * features * 6 * hidden_units, 34e6),
        name="middle",
    )(hidden, x, ct, w_in, w_out, vec, b_in)


def by_parity(step, run, even, odd):
    pl.when(step % 2 == 0)(lambda: run(even, odd))
    pl.when(step % 2 == 1)(lambda: run(odd, even))


def fill_copies(ext, left_hbm, own_hbm, right_hbm, sems):
    reach, own = left_hbm.shape[1], own_hbm.shape[1]
    return [
        pltpu.make_async_copy(own_hbm, ext.at[:, pl.ds(reach, own), :], sems.at[0]),
        pltpu.make_async_copy(left_hbm, ext.at[:, pl.ds(0, reach), :], sems.at[1]),
        pltpu.make_async_copy(right_hbm, ext.at[:, pl.ds(reach + own, reach), :], sems.at[2]),
    ]


def build_masked(lhs, ext, info_ref, tap, forward_masks, first=0):
    rows, extended, features = ext.shape
    taps = info_ref.shape[0] - 1
    reach = STEP * (taps // 2)
    own = extended - 2 * reach
    offset = STEP * tap if forward_masks else STEP * (taps - 1 - tap)
    ids = info_ref[0]
    moved = pltpu.roll(ids, extended - offset, 1)[:, :own]
    used = info_ref[1 + tap]
    if forward_masks:
        used = used[:, reach : reach + own]
    else:
        used = pltpu.roll(used, extended - offset, 1)[:, :own]
    columns = mask_columns((moved == ids[:, reach : reach + own]) & (used == 1))
    at = pl.ds(pl.multiple_of(offset, STEP), own)
    for r in range(rows):
        lhs[r * own : (r + 1) * own, :] = ext[r, at, :] * spread(
            columns[:, first + r : first + r + 1], features
        )


class Rider(NamedTuple):
    fn: Any
    operands: tuple
    in_specs: list
    out_specs: list
    out_shape: list
    steps: int


NO_RIDER = Rider(None, (), [], [], [], 0)


def ride(rider, step, ins, outs):
    if rider.fn is not None:
        pl.when(step < rider.steps)(lambda: rider.fn(ins, outs))


def rider_kernel(rider, *refs):
    count = len(rider.operands)
    rider.fn(refs[:count], refs[count:])


def alone(rider):
    moved = 3 * sum(v.size for v in rider.operands)
    return pl.pallas_call(
        functools.partial(rider_kernel, rider._replace(operands=(None,) * len(rider.operands))),
        grid=(rider.steps,),
        in_specs=rider.in_specs,
        out_specs=rider.out_specs,
        out_shape=rider.out_shape,
        compiler_params=params(8),
        cost_estimate=cost(moved / 2, moved),
        name="additions",
    )(*rider.operands)


def weight_kernel(blocks, rider, info_ref, gh_ref, x_hbm, left_hbm, right_hbm, *rest):
    ins, rest = rest[: len(rider.operands)], rest[len(rider.operands) :]
    if blocks == (1, 1):
        gw_ref, ext, lhs_even, lhs_odd, fill_sems = rest
        outs = ()
    else:
        keep_ref, send_ref, *rest = rest
        outs, rest = rest[: len(rider.out_shape)], rest[len(rider.out_shape) :]
        ext, lhs_even, lhs_odd, fill_sems, gw_ref, sems = rest
    tap = pl.program_id(0)
    taps = pl.num_programs(0)
    rows, own, features = gh_ref.shape

    @pl.when(tap == 0)
    def _():
        copies = fill_copies(ext, left_hbm, x_hbm, right_hbm, fill_sems)
        for copy in copies:
            copy.start()
        for copy in copies:
            copy.wait()
        build_masked(lhs_even, ext, info_ref, 0, True)

    n_wide, n_narrow = blocks
    height, width = features // n_narrow, features // n_wide
    rows_at = pl.ds(pl.multiple_of(tap * height, height), height)
    ride(rider, tap, ins, outs)

    def run(lhs, lhs_next):
        build_masked(lhs_next, ext, info_ref, jnp.minimum(tap + 1, taps - 1), True)
        product = dot(lhs[...], gh_ref[...].reshape(rows * own, features), 0, 0).astype(BF)
        for n in range(n_narrow):
            for w in range(n_wide):
                place_block(
                    gw_ref,
                    product[n * height : (n + 1) * height, w * width : (w + 1) * width],
                    w, n, rows_at, blocks,
                )

    by_parity(tap, run, lhs_even, lhs_odd)

    if blocks != (1, 1):

        def shipping(at):
            rows_of = pl.ds(pl.multiple_of(at * height, height), height)
            return [
                pltpu.make_async_copy(
                    gw_ref.at[i, :, rows_of, :], ref.at[:, rows_of, :], sems.at[i]
                )
                for i, ref in enumerate((keep_ref, send_ref))
            ]

        @pl.when(tap > 0)
        def _():
            for copy in shipping(tap - 1):
                copy.wait()

        for copy in shipping(tap):
            copy.start()

        @pl.when(tap == taps - 1)
        def _():
            for copy in shipping(tap):
                copy.wait()


def weight_gradient(blocks, info, gh, x, left, right, taps, rider=NO_RIDER):
    rows, own, features = x.shape
    reach = left.shape[1]
    shapes, specs, scratch = gradient_outputs(blocks, taps * features, features)
    light = rider._replace(operands=(None,) * len(rider.operands))
    return pl.pallas_call(
        functools.partial(weight_kernel, blocks, light),
        grid=(taps,),
        in_specs=[whole(info.shape), whole(gh.shape)]
        + [pl.BlockSpec(memory_space=pl.ANY)] * 3
        + rider.in_specs,
        out_specs=specs + rider.out_specs,
        out_shape=shapes + rider.out_shape,
        scratch_shapes=[
            pltpu.VMEM((rows, own + 2 * reach, features), BF),
            pltpu.VMEM((rows * own, features), BF),
            pltpu.VMEM((rows * own, features), BF),
            pltpu.SemaphoreType.DMA((3,)),
        ]
        + scratch,
        compiler_params=params(28),
        cost_estimate=cost(2 * rows * own * features * features * taps, 12e6),
        name="weight_gradient",
    )(info, gh, x, left, right, *rider.operands)


def input_kernel(first, rider, info_ref, w_ref, gh_hbm, left_hbm, right_hbm, gmixed_hbm, *rest):
    ins, rest = rest[: len(rider.operands)], rest[len(rider.operands) :]
    gx_hbm, *rest = rest
    outs, rest = rest[: len(rider.out_shape)], rest[len(rider.out_shape) :]
    ext, lhs_even, lhs_odd, acc, gmixed, fill_sems, in_sem, out_sems = rest
    tap = pl.program_id(0)
    taps = pl.num_programs(0)
    rows, own, features = gmixed.shape
    batch = pl.ds(first, rows)
    base = pltpu.make_async_copy(gmixed_hbm.at[batch], gmixed, in_sem)

    @pl.when(tap == 0)
    def _():
        copies = fill_copies(
            ext, left_hbm.at[batch], gh_hbm.at[batch], right_hbm.at[batch], fill_sems
        )
        for copy in copies:
            copy.start()
        base.start()
        acc[...] = jnp.zeros_like(acc)
        for copy in copies:
            copy.wait()
        build_masked(lhs_even, ext, info_ref, 0, False, first)

    ride(rider, tap, ins, outs)

    def run(lhs, lhs_next):
        build_masked(lhs_next, ext, info_ref, jnp.minimum(tap + 1, taps - 1), False, first)
        acc[...] += dot(lhs[...], w_ref[0], 1, 1)

    by_parity(tap, run, lhs_even, lhs_odd)

    @pl.when(tap == taps - 1)
    def _():
        base.wait()
        copies = []
        for r in range(rows):
            g_in = acc[r * own : (r + 1) * own, :].astype(BF).astype(F32)
            gmixed[r] = gmixed[r] + g_in
            copies.append(pltpu.make_async_copy(gmixed.at[r], gx_hbm.at[first + r], out_sems.at[r]))
            copies[-1].start()
        for copy in copies:
            copy.wait()


def input_gradient(info, conv_w, gh, left, right, gmixed, first, rows, rider=NO_RIDER):
    _, own, features = gh.shape
    reach = left.shape[1]
    taps = conv_w.shape[0]
    light = rider._replace(operands=(None,) * len(rider.operands))
    return pl.pallas_call(
        functools.partial(input_kernel, first, light),
        grid=(taps,),
        in_specs=[
            whole(info.shape),
            pl.BlockSpec((1, features, features), lambda i: (i, 0, 0)),
        ]
        + [pl.BlockSpec(memory_space=pl.ANY)] * 4
        + rider.in_specs,
        out_specs=[pl.BlockSpec(memory_space=pl.ANY)] + rider.out_specs,
        out_shape=[shape(gmixed.shape, F32)] + rider.out_shape,
        input_output_aliases={5: 0},
        scratch_shapes=[
            pltpu.VMEM((rows, own + 2 * reach, features), BF),
            pltpu.VMEM((rows * own, features), BF),
            pltpu.VMEM((rows * own, features), BF),
            pltpu.VMEM((rows * own, features), F32),
            pltpu.VMEM((rows, own, features), F32),
            pltpu.SemaphoreType.DMA((3,)),
            pltpu.SemaphoreType.DMA,
            pltpu.SemaphoreType.DMA((rows,)),
        ],
        compiler_params=params(20),
        cost_estimate=cost(2 * rows * own * features * features * taps, 12e6),
        name="input_gradient",
    )(info, conv_w, gh, left, right, gmixed, *rider.operands)


def flip(value, axis, bit):
    size = lax.axis_size(axis)
    return lax.ppermute(value, axis, [(i, i ^ bit) for i in range(size)])


def add(a, b):
    return a.astype(F32) + b.astype(F32)


def in_pair(value):
    high = value.astype(BF)
    return high, (value - high.astype(F32)).astype(BF)


def pair_sum(pair):
    return pair[0].astype(F32) + pair[1].astype(F32)


def stepwise(block, axis, steps):
    return pl.BlockSpec(
        block,
        lambda i: tuple(jnp.minimum(i, steps - 1) if d == axis else 0 for d in range(len(block))),
    )


def after_core(pairs, sums=()):
    count = len(pairs)
    half = sum(keep.shape[1] for keep, _ in pairs) // 2
    extra = 16 if sums else 0
    operands = [v.reshape((2, 2, 4) + v.shape[1:]) for side in zip(*pairs, strict=True) for v in side]

    def fn(ins, outs):
        a_keep, a_send, b_keep, b_send = outs
        base = 0
        for keep, got in zip(ins[:count], ins[count : 2 * count], strict=True):
            rows = keep.shape[3] // 2
            at = slice(base, base + rows)
            for y in range(2):
                for x in range(2):
                    total = add(keep[y, x, 0], got[y, x, 0]).astype(BF)
                    (a_send if x else a_keep)[y, 0, at, :] = total[:rows]
                    (b_send if y else b_keep)[x, 0, at, :] = total[rows:]
            base += rows
        if extra:
            high, low = in_pair(ins[-2][...] + ins[-1][...])
            for ref in (a_keep, a_send):
                ref[0, 0, half:, :] = high
                ref[1, 0, half:, :] = low

    tops = (2, 4, half + extra, 128), (2, 4, half + extra, 128), (2, 4, half, 128), (2, 4, half, 128)
    return Rider(
        fn,
        (*operands, *sums),
        [stepwise((2, 2, 1) + v.shape[3:], 2, 4) for v in operands]
        + [stepwise((16, 128), 0, 4) for _ in sums],
        [stepwise((2, 1) + d[2:], 1, 4) for d in tops],
        [shape(d, BF) for d in tops],
        4,
    )


def after_first(a_keep, a_got, b_keep, b_got):
    half = b_keep.shape[2]
    extra = a_keep.shape[2] - half

    def fn(ins, outs):
        a_keep, a_got, b_keep, b_got = ins
        a_next, a_send, b_next, b_send = outs
        for keep, got, stay, send in (
            (a_keep, a_got, a_next, a_send),
            (b_keep, b_got, b_next, b_send),
        ):
            stay[0, :half] = add(keep[0, 0, :half], got[0, 0, :half]).astype(BF)
            send[0, :half] = add(keep[1, 0, :half], got[1, 0, :half]).astype(BF)
        if extra:
            total = add(a_keep[0, 0, half:], a_keep[1, 0, half:]) + add(
                a_got[0, 0, half:], a_got[1, 0, half:]
            )
            high, low = in_pair(total)
            for ref in (a_next, a_send):
                ref[0, half : half + extra] = high
                ref[0, half + extra :] = low

    tops = [(4, half + 2 * extra, 128)] * 2 + [(4, half, 128)] * 2
    operands = (a_keep, a_got, b_keep, b_got)
    return Rider(
        fn,
        operands,
        [stepwise((2, 1) + v.shape[2:], 1, 4) for v in operands],
        [stepwise((1,) + d[1:], 0, 4) for d in tops],
        [shape(d, BF) for d in tops],
        4,
    )


def after_second_kernel(a_keep, a_got, b_keep, b_got, *outs):
    half = b_keep.shape[1]
    extra = (a_keep.shape[1] - half) // 2
    for i, ref in enumerate(outs):
        ref[0, :half] = add(a_keep[i, :half], a_got[i, :half]).astype(BF)
        ref[1, :half] = add(b_keep[i], b_got[i]).astype(BF)
    if extra:
        middle_at, end = half + extra, half + 2 * extra
        for z in range(4):
            total = add(a_keep[z, half:middle_at], a_keep[z, middle_at:end]) + add(
                a_got[z, half:middle_at], a_got[z, middle_at:end]
            )
            high, low = in_pair(total)
            at = slice(half + extra * z, half + extra * (z + 1))
            for ref in outs:
                ref[0, at] = high
                ref[1, at] = low


def after_second(a_keep, a_got, b_keep, b_got):
    half = b_keep.shape[1]
    rows = half + 2 * (a_keep.shape[1] - half)
    z = small(after_second_kernel, (a_keep, a_got, b_keep, b_got), [(2, rows, 128)] * 4)
    return (z[0], *(flip(z[i], "narrow", 2 * i) for i in (1, 2, 3)))


def last_ff_kernel(z0, z1, z2, z3, w_out_ref, w_in_ref, sums_ref):
    half = w_out_ref.shape[0] // 2
    height = w_in_ref.shape[0]
    count = w_in_ref.shape[1] // 128
    total = add(z0[...], z1[...]) + add(z2[...], z3[...])
    w_out_ref[:half] = total[0, :half]
    w_out_ref[half:] = total[1, :half]
    for j in range(count):
        side, at = divmod(j, count // 2)
        w_in_ref[:, 128 * j : 128 * (j + 1)] = total[side, half + at * height : half + (at + 1) * height]
    first = half + height * count // 2
    sums_ref[...] = total[0, first:] + total[1, first:]


def last_conv_kernel(z0, z1, z2, z3, out):
    total = add(z0[...], z1[...]) + add(z2[...], z3[...])
    half = total.shape[1]
    out[:half] = total[0]
    out[half:] = total[1]


def small(kernel, operands, dims, dtype=BF):
    moved = sum(v.size * v.dtype.itemsize for v in operands) * 2
    return pl.pallas_call(
        kernel,
        out_shape=[shape(d, dtype) for d in dims],
        compiler_params=params(12),
        cost_estimate=cost(moved / 2, moved),
        name=kernel.__name__,
    )(*operands)


def after(value, *others):
    return lax.optimization_barrier((value, others))[0]


def body(
    inputs, conv_w, conv_b, ln1_gain, ln1_bias, w_in, b_in, w_out, ln2_gain, ln2_bias,
    segments, tap_mask, cotangent,
):
    rows, own, features = inputs.shape
    taps = conv_w.shape[0]
    reach = STEP * (taps // 2)
    hidden_units = w_in.shape[1]
    n_wide, n_narrow = lax.axis_size("wide"), lax.axis_size("narrow")
    by_hand = (n_wide, n_narrow) == (4, 8)
    blocks = (4, 8) if by_hand else (1, 1)

    to_right = [(i, i + 1) for i in range(n_wide - 1)]
    to_left = [(i + 1, i) for i in range(n_wide - 1)]

    def halos(value, dim):
        last = value.shape[dim]
        left = lax.ppermute(lax.slice_in_dim(value, last - reach, last, axis=dim), "wide", to_right)
        right = lax.ppermute(lax.slice_in_dim(value, 0, reach, axis=dim), "wide", to_left)
        return left, right

    x_left, x_right = halos(inputs, 1)
    info = jnp.concatenate([segments[None] + 1, jnp.transpose(tap_mask, (1, 0, 2))], axis=0)
    info_left, info_right = halos(info, 2)
    info_ext = jnp.concatenate([info_left, info, info_right], axis=2)
    vec = jnp.stack([conv_b, ln1_gain, ln1_bias, ln2_gain, ln2_bias]).astype(F32)
    vec = jnp.pad(vec, ((0, 3), (0, 0)))

    acc = conv_inner(info, inputs, conv_w)
    hidden = conv_outer(info_ext, acc, x_left, x_right, conv_w, vec)
    out, gmixed, gh, sums, *grads = middle(
        blocks, hidden, inputs, cotangent, w_in, w_out, vec, b_in.astype(F32)[None]
    )
    gh_left, gh_right = halos(gh, 1)
    half_rows = rows // 2
    if not by_hand:
        gconv = weight_gradient(blocks, info_ext, gh, inputs, x_left, x_right, taps)
        gx = input_gradient(info_ext, conv_w, gh, gh_left, gh_right, gmixed, 0, half_rows)[0]
        gx = input_gradient(info_ext, conv_w, gh, gh_left, gh_right, gx, half_rows, half_rows)[0]

        def reduce(value, dims, wide_dim, narrow_dim):
            value = lax.psum_scatter(
                value.reshape(dims), "narrow", scatter_dimension=narrow_dim, tiled=True
            )
            return lax.psum_scatter(value, "wide", scatter_dimension=wide_dim, tiled=True).astype(
                F32
            )

        grad_w_out = reduce(grads[0], (hidden_units, features), 1, 0)
        grad_w_in = reduce(grads[1], (features, hidden_units), 1, 0)
        grad_conv = reduce(gconv[0], (taps, features, features), 2, 1)
        sums = lax.psum(sums, ("wide", "narrow"))
    else:
        got_out, got_in = flip(grads[1], "wide", 1), flip(grads[3], "wide", 1)
        got_sums = flip(sums, "wide", 1)
        rider = after_core(((grads[0], got_out), (grads[2], got_in)), (sums, got_sums))
        c_keep, c_send, *f = weight_gradient(
            blocks, info_ext, gh, inputs, x_left, x_right, taps, rider
        )
        c_send, f[1], f[3] = after((c_send, f[1], f[3]), gh_left, gh_right)
        c_got = flip(c_send, "wide", 1)
        f_got = flip(f[1], "narrow", 1), flip(f[3], "wide", 2)
        gx, *c = input_gradient(
            info_ext, conv_w, gh, gh_left, gh_right, gmixed, 0, half_rows,
            after_core(((c_keep, c_got),)),
        )
        c_got = flip(c[1], "narrow", 1), flip(c[3], "wide", 2)
        gx, *f = input_gradient(
            info_ext, conv_w, gh, gh_left, gh_right, gx, half_rows, half_rows,
            after_first(f[0], f_got[0], f[2], f_got[1]),
        )
        f_got = flip(f[1], "wide", 2), flip(f[3], "narrow", 1)
        c = after((c[0], c_got[0], c[2], c_got[1]), gx, f[1], f[3])
        c = alone(after_first(*c))
        c_got = flip(c[1], "wide", 2), flip(c[3], "narrow", 1)
        f = after_second(*after((f[0], f_got[0], f[2], f_got[1]), c[1], c[3]))
        c = after_second(*after((c[0], c_got[0], c[2], c_got[1]), f[0]))
        grad_w_out, grad_w_in, sums = small(
            last_ff_kernel, f,
            [
                (hidden_units // n_narrow, 128), (features // n_narrow, hidden_units // n_wide),
                sums.shape,
            ],
            F32,
        )
        grad_conv = small(last_conv_kernel, c, [(taps * features // n_narrow, 128)], F32)[0]
        grad_conv = grad_conv.reshape(taps, features // n_narrow, features // n_wide)
    sums = sums.reshape(-1)
    starts = [0, features, 2 * features, 3 * features]
    starts += [starts[-1] + hidden_units, starts[-1] + hidden_units + features]
    sizes = [features, features, features, hidden_units, features, features]
    vectors = [sums[a : a + n] for a, n in zip(starts, sizes, strict=True)]
    return (
        out, gx, grad_conv, vectors[0], vectors[1], vectors[2], grad_w_in, vectors[3],
        grad_w_out, vectors[4], vectors[5],
    )


def solution(mesh):
    split = P("narrow", "wide", None)
    placed = (split,) + (P(),) * 9 + (P("narrow", "wide"), P("narrow", None, "wide"), split)
    return jax.shard_map(
        body,
        mesh=mesh,
        in_specs=placed,
        out_specs=(
            split, split, P(None, "narrow", "wide"), P(), P(), P(), P("narrow", "wide"), P(),
            P("narrow", "wide"), P(), P(),
        ),
        check_vma=False,
    )
```

```python
import functools
from typing import Any, NamedTuple

import jax
import jax.numpy as jnp
from jax import lax
from jax.experimental import pallas as pl
from jax.experimental.pallas import tpu as pltpu
from jax.sharding import PartitionSpec as P

STEP = 32
BF = jnp.bfloat16
F32 = jnp.float32
RSQRT2 = 0.7071067811865476
RSQRT2PI = 0.3989422804014327
EPS = 1e-05


def params(mebibytes):
    return pltpu.CompilerParams(vmem_limit_bytes=mebibytes * 1024 * 1024)


def cost(flops, moved):
    return pl.CostEstimate(
        flops=int(flops / 50), bytes_accessed=int(moved / 50), transcendentals=0
    )


def whole(shape):
    rank = len(shape)
    return pl.BlockSpec(shape, lambda *_: (0,) * rank, pipeline_mode=pl.Buffered(1))


def shape(dims, dtype):
    return jax.ShapeDtypeStruct(dims, dtype)


def mask_columns(matched):
    return jnp.where(matched, 1.0, 0.0).astype(F32).T


def spread(column, width):
    wide = jnp.broadcast_to(column, (column.shape[0], 128)).astype(BF)
    return jnp.concatenate([wide] * (width // 128), axis=1)


def dot(left, right, left_dim, right_dim):
    return lax.dot_general(
        left, right, (((left_dim,), (right_dim,)), ((), ())), preferred_element_type=F32
    )


def cdf_and_exp(values):
    return 0.5 + 0.5 * lax.erf(values * RSQRT2), jnp.exp(-0.5 * values * values)


def in_pair(value):
    high = value.astype(BF)
    return high, (value - high.astype(F32)).astype(BF)


def fold(values):
    return values.reshape(-1, 8, values.shape[-1]).sum(0)


PACK_ROWS = 32


def pack_kernel(
    x_hbm, ids_hbm, used_hbm, left_ref, right_ref, info_ref, ids, sems, info_sems
):
    rows, own, features = x_hbm.shape
    count = info_ref.shape[0]
    reach = (left_ref.shape[0] - PACK_ROWS) // rows
    loads = [
        pltpu.make_async_copy(ids_hbm, ids, info_sems.at[0]),
        pltpu.make_async_copy(used_hbm, info_ref.at[pl.ds(1, count - 1)], info_sems.at[1]),
    ]
    for load in loads:
        load.start()
    copies = []
    for side, (out, start) in enumerate(((left_ref, 0), (right_ref, own - reach))):
        for r in range(rows):
            copies.append(
                pltpu.make_async_copy(
                    x_hbm.at[r, pl.ds(start, reach), :],
                    out.at[pl.ds(r * reach, reach), :],
                    sems.at[side * rows + r],
                )
            )
            copies[-1].start()
    for load in loads:
        load.wait()
    info_ref[0] = ids[...] + 1
    for side, (out, start) in enumerate(((left_ref, 0), (right_ref, own - reach))):
        lines = []
        for q in range(PACK_ROWS // rows):
            group = [
                info_ref[k, :, start : start + reach].astype(F32)
                if k < count
                else jnp.zeros((rows, reach), F32)
                for k in range(q * features // reach, (q + 1) * features // reach)
            ]
            lines.append(jnp.concatenate(group, axis=1))
        out[rows * reach :, :] = jnp.concatenate(lines, axis=0).astype(BF)
    for copy in copies:
        copy.wait()


def pack(x, ids, used, reach):
    rows, own, features = x.shape
    packed = shape((rows * reach + PACK_ROWS, features), BF)
    return pl.pallas_call(
        pack_kernel,
        grid=(1,),
        in_specs=[pl.BlockSpec(memory_space=pltpu.HBM)] * 3,
        out_specs=[whole(packed.shape)] * 2 + [whole((1 + used.shape[0], rows, own))],
        out_shape=[packed, packed, shape((1 + used.shape[0], rows, own), jnp.int32)],
        scratch_shapes=[
            pltpu.VMEM(ids.shape, jnp.int32),
            pltpu.SemaphoreType.DMA((2 * rows,)),
            pltpu.SemaphoreType.DMA((2,)),
        ],
        compiler_params=params(6),
        cost_estimate=cost(1e6, 4e6),
        name="pack",
    )(x, ids, used)


def put_masked(lhs, sources, columns, n, features):
    for r, source in enumerate(sources):
        lhs[r * n : (r + 1) * n, :] = source * spread(columns[:, r : r + 1], features)


def conv_inner_kernel(info_ref, x_ref, w_ref, acc_ref, even, odd):
    step = pl.program_id(0)
    rows, own, features = x_ref.shape
    taps = info_ref.shape[0] - 1
    half = taps // 2
    order = [half] + [k for k in range(taps) if k != half]
    buffers = (even, odd)

    def span(k):
        shift = STEP * (k - half)
        return max(0, -shift), own - max(0, shift), shift

    def build(i):
        k = order[i]
        low, high, shift = span(k)
        ids = info_ref[0]
        matched = (ids[:, low + shift : high + shift] == ids[:, low:high]) & (
            info_ref[1 + k][:, low:high] == 1
        )
        put_masked(
            buffers[i % 2],
            [x_ref[r, low + shift : high + shift, :] for r in range(rows)],
            mask_columns(matched), high - low, features,
        )

    def run(i):
        low, high, _ = span(order[i])
        n = high - low
        if i + 1 < taps:
            build(i + 1)
        product = dot(buffers[i % 2][: rows * n, :], w_ref[0], 1, 0).reshape(rows, n, features)
        if i == 0:
            acc_ref[...] = product
        else:
            acc_ref[:, low:high, :] += product

    pl.when(step == 0)(functools.partial(build, 0))
    for i in range(taps):
        pl.when(step == i)(functools.partial(run, i))


def conv_inner(info, x, conv_w):
    rows, own, features = x.shape
    taps = conv_w.shape[0]
    half = taps // 2

    def tap_of(i):
        return jnp.where(i == 0, half, jnp.where(i <= half, i - 1, i))

    return pl.pallas_call(
        conv_inner_kernel,
        grid=(taps,),
        in_specs=[
            whole(info.shape),
            whole(x.shape),
            pl.BlockSpec((1, features, features), lambda i: (tap_of(i), 0, 0)),
        ],
        out_specs=whole(x.shape),
        out_shape=shape(x.shape, F32),
        scratch_shapes=[pltpu.VMEM((rows * own, features), BF)] * 2,
        compiler_params=params(20),
        cost_estimate=cost(2 * rows * own * features * features * taps * 0.72, 11e6),
        name="conv_inner",
    )(info, x, conv_w)


def conv_outer_kernel(
    own_info_ref, left_ref, right_ref, w_ref, vec_ref, acc_hbm, hidden_ref, info_ref, acc, even, odd, sem
):
    step = pl.program_id(0)
    rows, own, features = hidden_ref.shape
    taps = info_ref.shape[0] - 1
    half = taps // 2
    reach = STEP * half
    order = [k for k in range(taps) if k != half]
    buffers = (even, odd)
    load = pltpu.make_async_copy(acc_hbm, acc, sem)

    def span(k):
        n = STEP * abs(k - half)
        return (0 if k < half else own - n), n

    def build(i):
        k = order[i]
        low, n = span(k)
        left = k < half
        source = reach - n if left else 0
        shift = -n if left else n
        at = reach + low
        ids = info_ref[0]
        matched = (info_ref[1 + k][:, at : at + n] == 1) & (
            ids[:, at + shift : at + shift + n] == ids[:, at : at + n]
        )
        halo = left_ref if left else right_ref
        put_masked(
            buffers[i % 2],
            [halo[r * reach + source : r * reach + source + n, :] for r in range(rows)],
            mask_columns(matched), n, features,
        )

    def run(i):
        low, n = span(order[i])
        if i + 1 < len(order):
            build(i + 1)
        product = dot(buffers[i % 2][: rows * n, :], w_ref[0], 1, 0).reshape(rows, n, features)
        acc[:, low : low + n, :] += product

    @pl.when(step == 0)
    def _():
        load.start()
        for halo, at in ((left_ref, 0), (right_ref, reach + own)):
            lines = halo[rows * reach :, :].astype(F32)
            for k in range(taps + 1):
                q, m = divmod(k, features // reach)
                part = lines[q * rows : (q + 1) * rows, m * reach : (m + 1) * reach]
                info_ref[k, :, at : at + reach] = part.astype(jnp.int32)
        info_ref[:, :, reach : reach + own] = own_info_ref[...]
        build(0)
        load.wait()

    for i in range(len(order)):
        pl.when(step == i)(functools.partial(run, i))

    @pl.when(step == len(order) - 1)
    def _():
        hidden_ref[...] = (acc[...] + vec_ref[0:1, :]).astype(BF)


def conv_outer(info, acc, left, right, conv_w, vec):
    rows, own, features = acc.shape
    taps = conv_w.shape[0]
    half = taps // 2
    reach = STEP * half
    info_dims = (1 + taps, rows, own + 2 * reach)
    return pl.pallas_call(
        conv_outer_kernel,
        grid=(taps - 1,),
        in_specs=[
            whole(info.shape),
            whole(left.shape),
            whole(right.shape),
            pl.BlockSpec((1, features, features), lambda i: (jnp.where(i < half, i, i + 1), 0, 0)),
            whole(vec.shape),
            pl.BlockSpec(memory_space=pl.ANY),
        ],
        out_specs=[whole(acc.shape), whole(info_dims)],
        out_shape=[shape(acc.shape, BF), shape(info_dims, jnp.int32)],
        scratch_shapes=[pltpu.VMEM(acc.shape, F32)]
        + [pltpu.VMEM((rows * reach, features), BF)] * 2
        + [pltpu.SemaphoreType.DMA],
        compiler_params=params(18),
        cost_estimate=cost(2 * rows * own * features * features * taps * 0.28, 11e6),
        name="conv_outer",
    )(info, left, right, conv_w, vec, acc)


def place_block(out_ref, value, dest_wide, dest_narrow, rows_at, blocks):
    if blocks == (1, 1):
        out_ref[0, 0, rows_at, :] = value
        return
    rel_wide = lax.axis_index("wide") ^ dest_wide
    rel_narrow = lax.axis_index("narrow") ^ dest_narrow
    index = (rel_wide >> 1) * 8 + (rel_narrow & 1) * 4 + (rel_narrow >> 1)
    out_ref[rel_wide & 1, index, rows_at, :] = value


def ship(pairs, sems):
    copies = [pltpu.make_async_copy(src, dst, sems.at[i]) for i, (src, dst) in enumerate(pairs)]
    for copy in copies:
        copy.start()
    for copy in copies:
        copy.wait()


def gradient_outputs(blocks, height, width):
    if blocks == (1, 1):
        dims = (1, 1, height, width)
        return [shape(dims, BF)], [whole(dims)], []
    n_wide, n_narrow = blocks
    height, width = height // n_narrow, width // n_wide
    dims = (n_wide * n_narrow // 2, height, width)
    return (
        [shape(dims, BF)] * 2,
        [pl.BlockSpec(memory_space=pl.ANY)] * 2,
        [pltpu.VMEM((2,) + dims, BF), pltpu.SemaphoreType.DMA((2,))],
    )


def moments(values):
    centered = values - jnp.mean(values, axis=1, keepdims=True)
    return centered, lax.rsqrt(jnp.mean(centered * centered, axis=1, keepdims=True) + EPS)


def middle_kernel(
    blocks,
    hidden_ref, x_ref, ct_ref, w_in_ref, w_out_ref, vec_ref, b_in_ref,
    out_ref, gmixed_ref, gh_ref, *rest,
):
    if blocks == (1, 1):
        gw_out_ref, gw_in_ref, sums_ref, *rest = rest
    else:
        keep_ref, send_ref, *rest = rest
    (
        act_scr, slope_scr, up_scr, gw_out_acc, gw_in_acc, b_in_acc, gain_one_acc,
        bias_one_acc, gain_two_acc, bias_two_acc, conv_b_acc, *rest,
    ) = rest
    if blocks != (1, 1):
        gw_ref, sums_ref, sems = rest
        gw_out_ref = gw_in_ref = gw_ref
    step = pl.program_id(0)
    steps = pl.num_programs(0)
    size = act_scr.shape[0]
    features, hidden_units = w_in_ref.shape

    @pl.when(step == 0)
    def _():
        for ref in (
            gw_out_acc, gw_in_acc, b_in_acc, gain_one_acc, bias_one_acc, gain_two_acc,
            bias_two_acc, conv_b_acc,
        ):
            ref[...] = jnp.zeros_like(ref)

    gain_one = vec_ref[1:2, :]
    bias_one = vec_ref[2:3, :]
    gain_two = vec_ref[3:4, :]
    bias_two = vec_ref[4:5, :]
    chunk = 512
    count = hidden_units // chunk
    pieces = [slice(j * chunk, (j + 1) * chunk) for j in range(count)]

    hid = hidden_ref[...].reshape(size, features).astype(F32)
    centered, scale = moments(hid * (0.5 + 0.5 * lax.erf(hid * RSQRT2)))
    mixed = x_ref[...].reshape(size, features).astype(F32) + (
        centered * scale * gain_one + bias_one
    )
    mixed_low = mixed.astype(BF)

    def up_part(cols):
        return dot(mixed_low, w_in_ref[:, cols], 1, 0) + b_in_ref[:, cols]

    projected = None
    up = up_part(pieces[0])
    for j, cols in enumerate(pieces):
        ahead = up_part(pieces[j + 1]) if j + 1 < count else None
        cdf, bell = cdf_and_exp(up)
        act_low = (up * cdf).astype(BF)
        slope_scr[:, cols] = cdf + up * bell * RSQRT2PI
        act_scr[:, cols] = act_low
        part = dot(act_low, w_out_ref[cols, :], 1, 0)
        projected = part if projected is None else projected + part
        up = ahead
    centered, scale = moments(projected)
    xhat = centered * scale
    out_ref[...] = (mixed + (xhat * gain_two + bias_two)).astype(BF).reshape(out_ref.shape)
    ct = ct_ref[...].reshape(size, features).astype(F32)
    gain_two_acc[...] += fold(ct * xhat)
    bias_two_acc[...] += fold(ct)
    e = ct * gain_two
    mean_e = jnp.mean(e, axis=1, keepdims=True)
    mean_ex = jnp.mean(e * xhat, axis=1, keepdims=True)
    gproj = (scale * (e - mean_e - xhat * mean_ex)).astype(BF)

    for cols in pieces:
        g_act = dot(gproj, w_out_ref[cols, :], 1, 1)
        up_low = (g_act * slope_scr[:, cols]).astype(BF)
        up_scr[:, cols] = up_low
        b_in_acc[:, cols] += fold(up_low.astype(F32))
    total = dot(up_scr[...], w_in_ref[...], 1, 1)
    for cols in pieces:
        gw_out_acc[cols, :] += dot(act_scr[:, cols], gproj, 0, 0)
        gw_in_acc[:, cols] += dot(mixed_low, up_scr[:, cols], 0, 0)
    g_mixed = ct_ref[...].reshape(size, features).astype(F32) + total
    gmixed_ref[...] = g_mixed.reshape(gmixed_ref.shape)
    hid = hidden_ref[...].reshape(size, features).astype(F32)
    cdf, bell = cdf_and_exp(hid)
    centered, scale = moments(hid * cdf)
    yhat = centered * scale
    gain_one_acc[...] += fold(g_mixed * yhat)
    bias_one_acc[...] += fold(g_mixed)
    e = g_mixed * gain_one
    mean_e = jnp.mean(e, axis=1, keepdims=True)
    mean_ey = jnp.mean(e * yhat, axis=1, keepdims=True)
    g_hidden = scale * (e - mean_e - yhat * mean_ey) * (cdf + hid * bell * RSQRT2PI)
    g_low = g_hidden.astype(BF)
    gh_ref[...] = g_low.reshape(gh_ref.shape)
    conv_b_acc[...] += fold(g_low.astype(F32))

    @pl.when(step == steps - 1)
    def _():
        row = 0
        for ref in (conv_b_acc, gain_one_acc, bias_one_acc, b_in_acc, gain_two_acc, bias_two_acc):
            summed = jnp.sum(ref[...], axis=0, keepdims=True)
            for j in range(ref.shape[1] // 128):
                sums_ref[row : row + 1, :] = summed[:, j * 128 : (j + 1) * 128]
                row += 1
        sums_ref[row:, :] = jnp.zeros_like(sums_ref[row:, :])
        n_wide, n_narrow = blocks
        height, width = features // n_narrow, hidden_units // n_wide
        lanes = gw_in_ref.shape[-1]
        base = 0 if blocks == (1, 1) else hidden_units // n_narrow
        for w in range(n_wide):
            product = gw_in_acc[:, w * width : (w + 1) * width].astype(BF)
            for n in range(n_narrow):
                for j in range(width // lanes):
                    place_block(
                        gw_in_ref,
                        product[n * height : (n + 1) * height, j * lanes : (j + 1) * lanes],
                        w, n, slice(base + j * height, base + (j + 1) * height), blocks,
                    )
        height, width = hidden_units // n_narrow, features // n_wide
        for n in range(n_narrow):
            product = gw_out_acc[n * height : (n + 1) * height, :].astype(BF)
            for w in range(n_wide):
                place_block(
                    gw_out_ref, product[:, w * width : (w + 1) * width], w, n, slice(0, height),
                    blocks,
                )
        if blocks != (1, 1):
            last = gw_ref.shape[2] - 16
            for i, part in enumerate(in_pair(sums_ref[...])):
                for j in range(4):
                    for side in range(2):
                        gw_ref[side, 4 * i + j, last:, :] = part[16 * j : 16 * (j + 1)]
            ship(((gw_ref.at[0], keep_ref), (gw_ref.at[1], send_ref)), sems)


def middle(blocks, hidden, x, ct, w_in, w_out, vec, b_in):
    rows, own, features = x.shape
    hidden_units = w_in.shape[1]
    block_rows = 2
    size = block_rows * own
    total = rows * own
    row_block = pl.BlockSpec((block_rows, own, features), lambda i: (i, 0, 0))
    sums = ((5 * features + hidden_units) // 128 + 63) // 64 * 64
    if blocks == (1, 1):
        dims = [(1, 1, hidden_units, features), (1, 1, features, hidden_units)]
        shapes = [shape(d, BF) for d in dims] + [shape((sums, 128), F32)]
        specs = [whole(v.shape) for v in shapes]
        scratch = []
    else:
        n_wide, n_narrow = blocks
        height = 2 * features * hidden_units // (n_wide * n_narrow * 128) + 16
        shapes = [shape((n_wide * n_narrow // 2, height, 128), BF)] * 2
        specs = [pl.BlockSpec(memory_space=pl.ANY)] * 2
        scratch = [
            pltpu.VMEM((2,) + shapes[0].shape, BF), pltpu.VMEM((sums, 128), F32),
            pltpu.SemaphoreType.DMA((2,)),
        ]
    narrow = pltpu.VMEM((8, features), F32)
    return pl.pallas_call(
        functools.partial(middle_kernel, blocks),
        grid=(rows // block_rows,),
        in_specs=[
            row_block, row_block, row_block, whole(w_in.shape), whole(w_out.shape),
            whole(vec.shape), whole(b_in.shape),
        ],
        out_specs=[row_block, row_block, row_block] + specs,
        out_shape=[shape(x.shape, BF), shape(x.shape, F32), shape(x.shape, BF)] + shapes,
        scratch_shapes=[
            pltpu.VMEM((size, hidden_units), BF), pltpu.VMEM((size, hidden_units), F32),
            pltpu.VMEM((size, hidden_units), BF),
            pltpu.VMEM((hidden_units, features), F32), pltpu.VMEM((features, hidden_units), F32),
            pltpu.VMEM((8, hidden_units), F32), narrow, narrow, narrow, narrow, narrow,
        ] + scratch,
        compiler_params=params(46),
        cost_estimate=cost(2 * total * features * 6 * hidden_units, 34e6),
        name="middle",
    )(hidden, x, ct, w_in, w_out, vec, b_in)


def by_parity(step, run, even, odd):
    pl.when(step % 2 == 0)(lambda: run(even, odd))
    pl.when(step % 2 == 1)(lambda: run(odd, even))


def fill_copies(ext, left_hbm, own_hbm, right_hbm, sems):
    rows, own = own_hbm.shape[0], own_hbm.shape[1]
    reach = (ext.shape[1] - own) // 2
    copies = [pltpu.make_async_copy(own_hbm, ext.at[:, pl.ds(reach, own), :], sems.at[0])]
    for side, (halo, at) in enumerate(((left_hbm, 0), (right_hbm, reach + own))):
        for r in range(rows):
            source = halo.at[r] if len(halo.shape) == 3 else halo.at[pl.ds(r * reach, reach), :]
            copies.append(
                pltpu.make_async_copy(
                    source, ext.at[r, pl.ds(at, reach), :], sems.at[1 + side * rows + r]
                )
            )
    return copies


def build_masked(lhs, ext, info_ref, tap, forward_masks, first=0):
    rows, extended, features = ext.shape
    taps = info_ref.shape[0] - 1
    reach = STEP * (taps // 2)
    own = extended - 2 * reach
    offset = STEP * tap if forward_masks else STEP * (taps - 1 - tap)
    ids = info_ref[0]
    moved = pltpu.roll(ids, extended - offset, 1)[:, :own]
    used = info_ref[1 + tap]
    if forward_masks:
        used = used[:, reach : reach + own]
    else:
        used = pltpu.roll(used, extended - offset, 1)[:, :own]
    columns = mask_columns((moved == ids[:, reach : reach + own]) & (used == 1))
    at = pl.ds(pl.multiple_of(offset, STEP), own)
    for r in range(rows):
        lhs[r * own : (r + 1) * own, :] = ext[r, at, :] * spread(
            columns[:, first + r : first + r + 1], features
        )


def weight_kernel(blocks, first, info_ref, gh_ref, x_hbm, left_hbm, right_hbm, *rest):
    if blocks == (1, 1):
        gw_ref, ext, lhs_even, lhs_odd, fill_sems = rest
    else:
        keep_ref, send_ref, ext, lhs_even, lhs_odd, fill_sems, gw_ref, sems = rest
    step = pl.program_id(0)
    steps = pl.num_programs(0)
    rows, own, features = gh_ref.shape

    @pl.when(step == 0)
    def _():
        copies = fill_copies(ext, left_hbm, x_hbm, right_hbm, fill_sems)
        for copy in copies:
            copy.start()
        for copy in copies:
            copy.wait()
        build_masked(lhs_even, ext, info_ref, first, True)

    n_wide, n_narrow = blocks
    height, width = features // n_narrow, features // n_wide
    rows_at = pl.ds(pl.multiple_of(step * height, height), height)

    def run(lhs, lhs_next):
        build_masked(lhs_next, ext, info_ref, first + jnp.minimum(step + 1, steps - 1), True)
        product = dot(lhs[...], gh_ref[...].reshape(rows * own, features), 0, 0).astype(BF)
        for n in range(n_narrow):
            for w in range(n_wide):
                place_block(
                    gw_ref,
                    product[n * height : (n + 1) * height, w * width : (w + 1) * width],
                    w, n, rows_at, blocks,
                )

    by_parity(step, run, lhs_even, lhs_odd)

    if blocks != (1, 1):

        def shipping(at):
            rows_of = pl.ds(pl.multiple_of(at * height, height), height)
            return [
                pltpu.make_async_copy(
                    gw_ref.at[i, :, rows_of, :], ref.at[:, rows_of, :], sems.at[i]
                )
                for i, ref in enumerate((keep_ref, send_ref))
            ]

        @pl.when(step > 0)
        def _():
            for copy in shipping(step - 1):
                copy.wait()

        for copy in shipping(step):
            copy.start()

        @pl.when(step == steps - 1)
        def _():
            for copy in shipping(step):
                copy.wait()


def weight_gradient(blocks, info, gh, x, left, right, first, taps):
    rows, own, features = x.shape
    shapes, specs, scratch = gradient_outputs(blocks, taps * features, features)
    return pl.pallas_call(
        functools.partial(weight_kernel, blocks, first),
        grid=(taps,),
        in_specs=[whole(info.shape), whole(gh.shape)] + [pl.BlockSpec(memory_space=pl.ANY)] * 3,
        out_specs=specs,
        out_shape=shapes,
        scratch_shapes=[
            pltpu.VMEM((rows, info.shape[2], features), BF),
            pltpu.VMEM((rows * own, features), BF),
            pltpu.VMEM((rows * own, features), BF),
            pltpu.SemaphoreType.DMA((1 + 2 * rows,)),
        ]
        + scratch,
        compiler_params=params(28),
        cost_estimate=cost(2 * rows * own * features * features * taps, 12e6),
        name="weight_gradient",
    )(info, gh, x, left, right)


def input_kernel(
    first, info_ref, w_ref, gh_hbm, left_hbm, right_hbm, gmixed_hbm,
    gx_hbm, ext, lhs_even, lhs_odd, acc, gmixed, fill_sems, in_sem, out_sems,
):
    tap = pl.program_id(0)
    taps = pl.num_programs(0)
    rows, own, features = gmixed.shape
    batch = pl.ds(first, rows)
    base = pltpu.make_async_copy(gmixed_hbm.at[batch], gmixed, in_sem)

    @pl.when(tap == 0)
    def _():
        copies = fill_copies(
            ext, left_hbm.at[batch], gh_hbm.at[batch], right_hbm.at[batch], fill_sems
        )
        for copy in copies:
            copy.start()
        base.start()
        acc[...] = jnp.zeros_like(acc)
        for copy in copies:
            copy.wait()
        build_masked(lhs_even, ext, info_ref, 0, False, first)

    def run(lhs, lhs_next):
        build_masked(lhs_next, ext, info_ref, jnp.minimum(tap + 1, taps - 1), False, first)
        acc[...] += dot(lhs[...], w_ref[0], 1, 1)

    by_parity(tap, run, lhs_even, lhs_odd)

    @pl.when(tap == taps - 1)
    def _():
        base.wait()
        copies = []
        for r in range(rows):
            g_in = acc[r * own : (r + 1) * own, :].astype(BF).astype(F32)
            gmixed[r] = gmixed[r] + g_in
            copies.append(pltpu.make_async_copy(gmixed.at[r], gx_hbm.at[first + r], out_sems.at[r]))
            copies[-1].start()
        for copy in copies:
            copy.wait()


def input_gradient(info, conv_w, gh, left, right, gmixed, first, rows):
    _, own, features = gh.shape
    reach = left.shape[1]
    taps = conv_w.shape[0]
    return pl.pallas_call(
        functools.partial(input_kernel, first),
        grid=(taps,),
        in_specs=[
            whole(info.shape),
            pl.BlockSpec((1, features, features), lambda i: (i, 0, 0)),
        ]
        + [pl.BlockSpec(memory_space=pl.ANY)] * 4,
        out_specs=pl.BlockSpec(memory_space=pl.ANY),
        out_shape=shape(gmixed.shape, F32),
        input_output_aliases={5: 0},
        scratch_shapes=[
            pltpu.VMEM((rows, own + 2 * reach, features), BF),
            pltpu.VMEM((rows * own, features), BF),
            pltpu.VMEM((rows * own, features), BF),
            pltpu.VMEM((rows * own, features), F32),
            pltpu.VMEM((rows, own, features), F32),
            pltpu.SemaphoreType.DMA((1 + 2 * rows,)),
            pltpu.SemaphoreType.DMA,
            pltpu.SemaphoreType.DMA((rows,)),
        ],
        compiler_params=params(20),
        cost_estimate=cost(2 * rows * own * features * features * taps, 12e6),
        name="input_gradient",
    )(info, conv_w, gh, left, right, gmixed)


class Additions(NamedTuple):
    fn: Any
    operands: tuple
    in_specs: list
    out_specs: list
    out_shape: list
    steps: int


def additions_kernel(fn, count, *refs):
    fn(refs[:count], refs[count:])


def alone(work):
    moved = 3 * sum(v.size for v in work.operands)
    return pl.pallas_call(
        functools.partial(additions_kernel, work.fn, len(work.operands)),
        grid=(work.steps,),
        in_specs=work.in_specs,
        out_specs=work.out_specs,
        out_shape=work.out_shape,
        compiler_params=params(8),
        cost_estimate=cost(moved / 2, moved),
        name="additions",
    )(*work.operands)


def flip(value, axis, bit):
    size = lax.axis_size(axis)
    return lax.ppermute(value, axis, [(i, i ^ bit) for i in range(size)])


def add(a, b):
    return a.astype(F32) + b.astype(F32)


def stepwise(block, axis):
    return pl.BlockSpec(block, lambda i: tuple(i if d == axis else 0 for d in range(len(block))))


def after_core(keep, got, top, extra=0):
    end = keep.shape[1] - extra
    operands = [v.reshape((2, 2, 4) + v.shape[1:]) for v in (keep, got)]

    def fn(ins, outs):
        a_keep, a_send, b_keep, b_send = outs
        keep, got = ins
        for y in range(2):
            for x in range(2):
                total = add(keep[y, x, 0, :end], got[y, x, 0, :end]).astype(BF)
                (a_send if x else a_keep)[y, 0, :top, :] = total[:top]
                (b_send if y else b_keep)[x, 0, :, :] = total[top:]
        if extra:
            total = add(keep[0, 0, 0, end:], keep[0, 1, 0, end:]) + add(
                got[0, 0, 0, end:], got[0, 1, 0, end:]
            )
            for i, part in enumerate(in_pair(total)):
                for ref in (a_keep, a_send):
                    ref[i, 0, top:, :] = part

    dims = [(2, 4, top + extra, 128)] * 2 + [(2, 4, end - top, 128)] * 2
    return Additions(
        fn,
        tuple(operands),
        [stepwise((2, 2, 1) + v.shape[3:], 2) for v in operands],
        [stepwise((2, 1) + d[2:], 1) for d in dims],
        [shape(d, BF) for d in dims],
        4,
    )


def after_first(top, a_keep, a_got, b_keep, b_got):
    extra = a_keep.shape[2] - top

    def fn(ins, outs):
        a_keep, a_got, b_keep, b_got = ins
        a_next, a_send, b_next, b_send = outs
        for keep, got, stay, send in (
            (a_keep, a_got, a_next, a_send),
            (b_keep, b_got, b_next, b_send),
        ):
            n = stay.shape[1] if stay is b_next else top
            stay[0, :n] = add(keep[0, 0, :n], got[0, 0, :n]).astype(BF)
            send[0, :n] = add(keep[1, 0, :n], got[1, 0, :n]).astype(BF)
        if extra:
            total = add(a_keep[0, 0, top:], a_keep[1, 0, top:]) + add(
                a_got[0, 0, top:], a_got[1, 0, top:]
            )
            for i, part in enumerate(in_pair(total)):
                for ref in (a_next, a_send):
                    ref[0, top + i * extra : top + (i + 1) * extra] = part

    dims = [(4, top + 2 * extra, 128)] * 2 + [(4, b_keep.shape[2], 128)] * 2
    operands = (a_keep, a_got, b_keep, b_got)
    return Additions(
        fn,
        operands,
        [stepwise((2, 1) + v.shape[2:], 1) for v in operands],
        [stepwise((1,) + d[1:], 0) for d in dims],
        [shape(d, BF) for d in dims],
        4,
    )


def after_second_kernel(top, a_keep, a_got, b_keep, b_got, *outs):
    extra = (a_keep.shape[1] - top) // 2
    end = top + b_keep.shape[1]
    for i, ref in enumerate(outs):
        ref[:top] = add(a_keep[i, :top], a_got[i, :top]).astype(BF)
        ref[top:end] = add(b_keep[i], b_got[i]).astype(BF)
    if extra:
        for z in range(4):
            high, low = slice(top, top + extra), slice(top + extra, top + 2 * extra)
            total = add(a_keep[z, high], a_keep[z, low]) + add(a_got[z, high], a_got[z, low])
            for i, part in enumerate(in_pair(total)):
                at = end + (4 * i + z) * extra
                for ref in outs:
                    ref[at : at + extra] = part


def after_second(top, a_keep, a_got, b_keep, b_got):
    rows = top + b_keep.shape[1] + 4 * (a_keep.shape[1] - top)
    z = small(
        functools.partial(after_second_kernel, top),
        (a_keep, a_got, b_keep, b_got), [(rows, 128)] * 4,
    )
    return (z[0], *(flip(z[i], "narrow", 2 * i) for i in (1, 2, 3)))


def last_ff_kernel(z0, z1, z2, z3, w_out_ref, w_in_ref, sums_ref):
    out_rows, (height, width) = w_out_ref.shape[0], w_in_ref.shape
    total = add(z0[...], z1[...]) + add(z2[...], z3[...])
    w_out_ref[...] = total[:out_rows]
    for j in range(width // 128):
        at = out_rows + j * height
        w_in_ref[:, 128 * j : 128 * (j + 1)] = total[at : at + height]
    end = out_rows + height * width // 128
    rows = sums_ref.shape[0]
    sums_ref[...] = total[end : end + rows] + total[end + rows :]


def last_conv_kernel(z0, z1, z2, z3, out):
    out[...] = add(z0[...], z1[...]) + add(z2[...], z3[...])


def small(kernel, operands, dims, dtype=BF):
    moved = sum(v.size * v.dtype.itemsize for v in operands) * 2
    return pl.pallas_call(
        kernel,
        out_shape=[shape(d, dtype) for d in dims],
        compiler_params=params(12),
        cost_estimate=cost(moved / 2, moved),
        name="additions",
    )(*operands)


def after(value, *others):
    return lax.optimization_barrier((value, others))[0]


def body(
    inputs, conv_w, conv_b, ln1_gain, ln1_bias, w_in, b_in, w_out, ln2_gain, ln2_bias,
    segments, tap_mask, cotangent,
):
    rows, own, features = inputs.shape
    taps = conv_w.shape[0]
    reach = STEP * (taps // 2)
    hidden_units = w_in.shape[1]
    n_wide, n_narrow = lax.axis_size("wide"), lax.axis_size("narrow")
    by_hand = (n_wide, n_narrow) == (4, 8)
    blocks = (4, 8) if by_hand else (1, 1)

    to_right = [(i, i + 1) for i in range(n_wide - 1)]
    to_left = [(i + 1, i) for i in range(n_wide - 1)]

    def halos(value, dim):
        last = value.shape[dim]
        left = lax.ppermute(lax.slice_in_dim(value, last - reach, last, axis=dim), "wide", to_right)
        right = lax.ppermute(lax.slice_in_dim(value, 0, reach, axis=dim), "wide", to_left)
        return left, right

    in_place = functools.partial(pltpu.with_memory_space_constraint, memory_space=pltpu.HBM)
    to_send_left, to_send_right, info = pack(
        in_place(inputs), in_place(segments), in_place(jnp.transpose(tap_mask, (1, 0, 2))), reach
    )
    x_left = lax.ppermute(to_send_right, "wide", to_right)
    x_right = lax.ppermute(to_send_left, "wide", to_left)
    vec = jnp.stack([conv_b, ln1_gain, ln1_bias, ln2_gain, ln2_bias]).astype(F32)
    vec = jnp.pad(vec, ((0, 3), (0, 0)))

    acc = conv_inner(info, in_place(inputs), in_place(conv_w))
    hidden, info = conv_outer(info, acc, x_left, x_right, conv_w, vec)
    out, gmixed, gh, *grads = middle(
        blocks, hidden, inputs, cotangent, w_in, w_out, vec, b_in.astype(F32)[None]
    )
    if not by_hand:
        gh_left, gh_right = halos(gh, 1)
        gconv = weight_gradient(blocks, info, gh, inputs, x_left, x_right, 0, taps)
        gx = input_gradient(info, conv_w, gh, gh_left, gh_right, gmixed, 0, rows)

        def reduce(value, dims, wide_dim, narrow_dim):
            value = lax.psum_scatter(
                value.reshape(dims), "narrow", scatter_dimension=narrow_dim, tiled=True
            )
            return lax.psum_scatter(value, "wide", scatter_dimension=wide_dim, tiled=True).astype(
                F32
            )

        grad_w_out = reduce(grads[0], (hidden_units, features), 1, 0)
        grad_w_in = reduce(grads[1], (features, hidden_units), 1, 0)
        grad_conv = reduce(gconv[0], (taps, features, features), 2, 1)
        sums = lax.psum(grads[2], ("wide", "narrow"))
    else:
        together = lax.optimization_barrier
        cuts = (0, rows // 4, rows - rows // 4, rows)

        def inputs_part(i, gx):
            first, end = cuts[i], cuts[i + 1]
            return input_gradient(info, conv_w, gh, gh_left, gh_right, gx, first, end - first)

        height = features // n_narrow
        f_top = (grads[0].shape[1] - 16) * 3 // 4 // 16 * 16
        c_top = taps * height // 2 // 16 * 16
        f_got = flip(grads[1], "wide", 1)
        gh_left, gh_right = halos(gh, 1)
        f = alone(after_core(grads[0], f_got, f_top, 16))
        f_got = flip(f[1], "narrow", 1), flip(f[3], "wide", 2)
        c = weight_gradient(blocks, info, after(gh, *f), inputs, x_left, x_right, 0, taps)

        c, f, f_got, gh_left, gh_right = together((c, f, f_got, gh_left, gh_right))
        c_got = flip(c[1], "wide", 1)
        f = alone(after_first(f_top, f[0], f_got[0], f[2], f_got[1]))
        f_got = flip(f[1], "wide", 2), flip(f[3], "narrow", 1)
        gx = inputs_part(0, after(gmixed, *f))

        gx, c, c_got, f, f_got = together((gx, c[0], c_got, f, f_got))
        c = alone(after_core(c, c_got, c_top))
        c_got = flip(c[1], "narrow", 1), flip(c[3], "wide", 2)
        f = after_second(f_top, *after((f[0], f_got[0], f[2], f_got[1]), *c))
        gx = inputs_part(1, after(gx, *c, f[0]))

        gx, c, c_got, f = together((gx, c, c_got, f))
        c = alone(after_first(c_top, c[0], c_got[0], c[2], c_got[1]))
        c_got = flip(c[1], "wide", 2), flip(c[3], "narrow", 1)
        gx = inputs_part(2, after(gx, *c))

        gx, c, c_got, f = together((gx, c, c_got, f))
        c = after_second(c_top, c[0], c_got[0], c[2], c_got[1])
        f = after(f, c[0])
        grad_w_out, grad_w_in, sums = small(
            last_ff_kernel, f,
            [(hidden_units // n_narrow, 128), (height, hidden_units // n_wide), (64, 128)],
            F32,
        )
        grad_conv = small(last_conv_kernel, c, [(taps * height, 128)], F32)[0]
        grad_conv = grad_conv.reshape(taps, height, features // n_wide)
    sums = sums.reshape(-1)
    starts = [0, features, 2 * features, 3 * features]
    starts += [starts[-1] + hidden_units, starts[-1] + hidden_units + features]
    sizes = [features, features, features, hidden_units, features, features]
    vectors = [sums[a : a + n] for a, n in zip(starts, sizes, strict=True)]
    return (
        out, gx, grad_conv, vectors[0], vectors[1], vectors[2], grad_w_in, vectors[3],
        grad_w_out, vectors[4], vectors[5],
    )


def solution(mesh):
    split = P("narrow", "wide", None)
    placed = (split,) + (P(),) * 9 + (P("narrow", "wide"), P("narrow", None, "wide"), split)
    return jax.shard_map(
        body,
        mesh=mesh,
        in_specs=placed,
        out_specs=(
            split, split, P(None, "narrow", "wide"), P(), P(), P(), P("narrow", "wide"), P(),
            P("narrow", "wide"), P(), P(),
        ),
        check_vma=False,
    )
```

```python
import functools
from typing import Any, NamedTuple

import jax
import jax.numpy as jnp
from jax import lax
from jax.experimental import pallas as pl
from jax.experimental.pallas import tpu as pltpu
from jax.sharding import PartitionSpec as P

STEP = 32
BF = jnp.bfloat16
F32 = jnp.float32
RSQRT2 = 0.7071067811865476
RSQRT2PI = 0.3989422804014327
EPS = 1e-05


def params(mebibytes):
    return pltpu.CompilerParams(vmem_limit_bytes=mebibytes * 1024 * 1024)


def cost(flops, moved):
    return pl.CostEstimate(
        flops=int(flops / 50), bytes_accessed=int(moved / 50), transcendentals=0
    )


def whole(shape):
    rank = len(shape)
    return pl.BlockSpec(shape, lambda *_: (0,) * rank, pipeline_mode=pl.Buffered(1))


def shape(dims, dtype):
    return jax.ShapeDtypeStruct(dims, dtype)


def mask_columns(matched):
    return jnp.where(matched, 1.0, 0.0).astype(F32).T


def spread(column, width):
    wide = jnp.broadcast_to(column, (column.shape[0], 128)).astype(BF)
    return jnp.concatenate([wide] * (width // 128), axis=1)


def dot(left, right, left_dim, right_dim):
    return lax.dot_general(
        left, right, (((left_dim,), (right_dim,)), ((), ())), preferred_element_type=F32
    )


def cdf_and_exp(values):
    return 0.5 + 0.5 * lax.erf(values * RSQRT2), jnp.exp(-0.5 * values * values)


def in_pair(value):
    high = value.astype(BF)
    return high, (value - high.astype(F32)).astype(BF)


def fold(values):
    return values.reshape(-1, 8, values.shape[-1]).sum(0)


def pair_sides():
    odd = lax.axis_index("wide") % 2
    return 1 - odd, odd


PACK_ROWS = 32


def pack_kernel(
    x_hbm, ids_hbm, used_hbm, near_ref, far_ref, info_ref, ids, sems, info_sems
):
    rows, own, features = x_hbm.shape
    count = info_ref.shape[0]
    reach = (near_ref.shape[0] - PACK_ROWS) // rows
    near, far = pair_sides()
    ends = tuple(
        (ref, pl.multiple_of(side * (own - reach), reach)) for ref, side in ((near_ref, near), (far_ref, far))
    )
    loads = [
        pltpu.make_async_copy(ids_hbm, ids, info_sems.at[0]),
        pltpu.make_async_copy(used_hbm, info_ref.at[pl.ds(1, count - 1)], info_sems.at[1]),
    ]
    for load in loads:
        load.start()
    copies = []
    for side, (out, start) in enumerate(ends):
        for r in range(rows):
            copies.append(
                pltpu.make_async_copy(
                    x_hbm.at[r, pl.ds(start, reach), :],
                    out.at[pl.ds(r * reach, reach), :],
                    sems.at[side * rows + r],
                )
            )
            copies[-1].start()
    for load in loads:
        load.wait()
    info_ref[0] = ids[...] + 1
    for side, (out, start) in enumerate(ends):
        lines = []
        for q in range(PACK_ROWS // rows):
            group = [
                info_ref[k, :, pl.ds(start, reach)].astype(F32)
                if k < count
                else jnp.zeros((rows, reach), F32)
                for k in range(q * features // reach, (q + 1) * features // reach)
            ]
            lines.append(jnp.concatenate(group, axis=1))
        out[rows * reach :, :] = jnp.concatenate(lines, axis=0).astype(BF)
    for copy in copies:
        copy.wait()


def pack(x, ids, used, reach):
    rows, own, features = x.shape
    packed = shape((rows * reach + PACK_ROWS, features), BF)
    return pl.pallas_call(
        pack_kernel,
        grid=(1,),
        in_specs=[pl.BlockSpec(memory_space=pltpu.HBM)] * 3,
        out_specs=[whole(packed.shape)] * 2 + [whole((1 + used.shape[0], rows, own))],
        out_shape=[packed, packed, shape((1 + used.shape[0], rows, own), jnp.int32)],
        scratch_shapes=[
            pltpu.VMEM(ids.shape, jnp.int32),
            pltpu.SemaphoreType.DMA((2 * rows,)),
            pltpu.SemaphoreType.DMA((2,)),
        ],
        compiler_params=params(6),
        cost_estimate=cost(1e6, 4e6),
        name="pack",
    )(x, ids, used)


def put_masked(lhs, sources, columns, n, features):
    for r, source in enumerate(sources):
        lhs[r * n : (r + 1) * n, :] = source * spread(columns[:, r : r + 1], features)


def conv_inner_kernel(info_ref, x_ref, w_ref, acc_ref, even, odd):
    step = pl.program_id(0)
    rows, own, features = x_ref.shape
    taps = info_ref.shape[0] - 1
    half = taps // 2
    order = [half] + [k for k in range(taps) if k != half]
    buffers = (even, odd)

    def span(k):
        shift = STEP * (k - half)
        return max(0, -shift), own - max(0, shift), shift

    def build(i):
        k = order[i]
        low, high, shift = span(k)
        ids = info_ref[0]
        matched = (ids[:, low + shift : high + shift] == ids[:, low:high]) & (
            info_ref[1 + k][:, low:high] == 1
        )
        put_masked(
            buffers[i % 2],
            [x_ref[r, low + shift : high + shift, :] for r in range(rows)],
            mask_columns(matched), high - low, features,
        )

    def run(i):
        low, high, _ = span(order[i])
        n = high - low
        if i + 1 < taps:
            build(i + 1)
        product = dot(buffers[i % 2][: rows * n, :], w_ref[0], 1, 0).reshape(rows, n, features)
        if i == 0:
            acc_ref[...] = product
        else:
            acc_ref[:, low:high, :] += product

    pl.when(step == 0)(functools.partial(build, 0))
    for i in range(taps):
        pl.when(step == i)(functools.partial(run, i))


def conv_inner(info, x, conv_w):
    rows, own, features = x.shape
    taps = conv_w.shape[0]
    half = taps // 2

    def tap_of(i):
        return jnp.where(i == 0, half, jnp.where(i <= half, i - 1, i))

    return pl.pallas_call(
        conv_inner_kernel,
        grid=(taps,),
        in_specs=[
            whole(info.shape),
            whole(x.shape),
            pl.BlockSpec((1, features, features), lambda i: (tap_of(i), 0, 0)),
        ],
        out_specs=whole(x.shape),
        out_shape=shape(x.shape, F32),
        scratch_shapes=[pltpu.VMEM((rows * own, features), BF)] * 2,
        compiler_params=params(12),
        cost_estimate=cost(2 * rows * own * features * features * taps * 0.72, 11e6),
        name="conv_inner",
    )(info, x, conv_w)


def conv_outer_kernel(
    own_info_ref, near_hbm, far_hbm, low_w_ref, high_w_ref, vec_ref, acc_hbm,
    hidden_ref, info_ref, acc, *rest,
):
    even, odd, (halos, sem, halo_sems) = rest[:2], rest[2:4], rest[4:]
    step = pl.program_id(0)
    rows, own, features = hidden_ref.shape
    taps = info_ref.shape[0] - 1
    half = taps // 2
    reach = STEP * half
    buffers = ((even[0], even[1]), (odd[0], odd[1]))
    load = pltpu.make_async_copy(acc_hbm, acc, sem)

    def span(k):
        n = STEP * abs(k - half)
        return (0 if k < half else own - n), n

    def sides(i):
        return (i, low_w_ref, 0), (taps - 1 - i, high_w_ref, 1)

    def build(i):
        for k, _, side in sides(i):
            low, n = span(k)
            source = 0 if side else reach - n
            at = reach + low
            shift = n if side else -n
            ids = info_ref[0]
            matched = (info_ref[1 + k][:, at : at + n] == 1) & (
                ids[:, at + shift : at + shift + n] == ids[:, at : at + n]
            )
            put_masked(
                buffers[i % 2][side],
                [halos[side, r * reach + source : r * reach + source + n, :] for r in range(rows)],
                mask_columns(matched), n, features,
            )

    def run(i):
        if i + 1 < half:
            build(i + 1)
        for k, w_ref, side in sides(i):
            low, n = span(k)
            product = dot(buffers[i % 2][side][: rows * n, :], w_ref[0], 1, 0)
            acc[:, low : low + n, :] += product.reshape(rows, n, features)

    @pl.when(step == 0)
    def _():
        copies = [
            pltpu.make_async_copy(src, halos.at[side], halo_sems.at[i])
            for i, (src, side) in enumerate(zip((near_hbm, far_hbm), pair_sides(), strict=True))
        ]
        for copy in copies:
            copy.start()
        load.start()
        for copy in copies:
            copy.wait()
        for side, at in enumerate((0, reach + own)):
            lines = halos[side, rows * reach :, :].astype(F32)
            for k in range(taps + 1):
                q, m = divmod(k, features // reach)
                part = lines[q * rows : (q + 1) * rows, m * reach : (m + 1) * reach]
                info_ref[k, :, at : at + reach] = part.astype(jnp.int32)
        info_ref[:, :, reach : reach + own] = own_info_ref[...]
        build(0)
        load.wait()

    for i in range(half):
        pl.when(step == i)(functools.partial(run, i))

    @pl.when(step == half - 1)
    def _():
        hidden_ref[...] = (acc[...] + vec_ref[0:1, :]).astype(BF)


def conv_outer(info, acc, near, far, conv_w, vec):
    rows, own, features = acc.shape
    taps = conv_w.shape[0]
    half = taps // 2
    reach = STEP * half
    info_dims = (1 + taps, rows, own + 2 * reach)
    return pl.pallas_call(
        conv_outer_kernel,
        grid=(half,),
        in_specs=[
            whole(info.shape),
            pl.BlockSpec(memory_space=pl.ANY),
            pl.BlockSpec(memory_space=pl.ANY),
            pl.BlockSpec((1, features, features), lambda i: (i, 0, 0)),
            pl.BlockSpec((1, features, features), lambda i: (taps - 1 - i, 0, 0)),
            whole(vec.shape),
            pl.BlockSpec(memory_space=pl.ANY),
        ],
        out_specs=[whole(acc.shape), whole(info_dims)],
        out_shape=[shape(acc.shape, BF), shape(info_dims, jnp.int32)],
        scratch_shapes=[pltpu.VMEM(acc.shape, F32)]
        + [pltpu.VMEM((rows * reach, features), BF)] * 4
        + [
            pltpu.VMEM((2,) + near.shape, BF),
            pltpu.SemaphoreType.DMA,
            pltpu.SemaphoreType.DMA((2,)),
        ],
        compiler_params=params(14),
        cost_estimate=cost(2 * rows * own * features * features * taps * 0.28, 11e6),
        name="conv_outer",
    )(info, near, far, conv_w, conv_w, vec, acc)


def place_block(out_ref, value, dest_wide, dest_narrow, rows_at, blocks):
    if blocks == (1, 1):
        out_ref[0, 0, rows_at, :] = value
        return
    rel_wide = lax.axis_index("wide") ^ dest_wide
    rel_narrow = lax.axis_index("narrow") ^ dest_narrow
    index = (rel_wide >> 1) * 8 + (rel_narrow & 1) * 4 + (rel_narrow >> 1)
    out_ref[rel_wide & 1, index, rows_at, :] = value


def gradient_outputs(blocks, height, width):
    if blocks == (1, 1):
        dims = (1, 1, height, width)
        return [shape(dims, BF)], [whole(dims)], []
    n_wide, n_narrow = blocks
    height, width = height // n_narrow, width // n_wide
    dims = (n_wide * n_narrow // 2, height, width)
    return (
        [shape(dims, BF)] * 2,
        [pl.BlockSpec(memory_space=pl.ANY)] * 2,
        [pltpu.VMEM((2,) + dims, BF), pltpu.SemaphoreType.DMA((2,))],
    )


def moments(values):
    centered = values - jnp.mean(values, axis=1, keepdims=True)
    return centered, lax.rsqrt(jnp.mean(centered * centered, axis=1, keepdims=True) + EPS)


def middle_kernel(
    blocks,
    hidden_ref, x_ref, ct_ref, w_in_hbm, w_out_hbm, vec_ref, b_in_ref,
    out_ref, gmixed_ref, gh_ref, *rest,
):
    if blocks == (1, 1):
        gw_out_ref, gw_in_ref, sums_ref, *rest = rest
    else:
        keep_ref, send_ref, *rest = rest
    (
        w_in_ref, w_out_ref, load_sems, act_scr, slope_scr, up_scr, gw_out_acc, gw_in_acc, b_in_acc, gain_one_acc,
        bias_one_acc, gain_two_acc, bias_two_acc, conv_b_acc, *rest,
    ) = rest
    if blocks != (1, 1):
        gw_ref, sums_ref, sems = rest
        gw_out_ref = gw_in_ref = gw_ref
    step = pl.program_id(0)
    steps = pl.num_programs(0)
    size = act_scr.shape[0]
    features, hidden_units = w_in_ref.shape
    loads = [
        pltpu.make_async_copy(src, dst, load_sems.at[i])
        for i, (src, dst) in enumerate(((w_in_hbm, w_in_ref), (w_out_hbm, w_out_ref)))
    ]

    @pl.when(step == 0)
    def _():
        for load in loads:
            load.start()
        for ref in (
            b_in_acc, gain_one_acc, bias_one_acc, gain_two_acc, bias_two_acc, conv_b_acc,
        ):
            ref[...] = jnp.zeros_like(ref)
        for load in loads:
            load.wait()

    gain_one = vec_ref[1:2, :]
    bias_one = vec_ref[2:3, :]
    gain_two = vec_ref[3:4, :]
    bias_two = vec_ref[4:5, :]
    chunk = 512
    count = hidden_units // chunk
    pieces = [slice(j * chunk, (j + 1) * chunk) for j in range(count)]

    hid = hidden_ref[...].reshape(size, features).astype(F32)
    centered, scale = moments(hid * (0.5 + 0.5 * lax.erf(hid * RSQRT2)))
    mixed = x_ref[...].reshape(size, features).astype(F32) + (
        centered * scale * gain_one + bias_one
    )
    mixed_low = mixed.astype(BF)

    def up_part(cols):
        return dot(mixed_low, w_in_ref[:, cols], 1, 0) + b_in_ref[:, cols]

    projected = None
    up = up_part(pieces[0])
    for j, cols in enumerate(pieces):
        ahead = up_part(pieces[j + 1]) if j + 1 < count else None
        cdf, bell = cdf_and_exp(up)
        act_low = (up * cdf).astype(BF)
        slope_scr[:, cols] = cdf + up * bell * RSQRT2PI
        act_scr[:, cols] = act_low
        part = dot(act_low, w_out_ref[cols, :], 1, 0)
        projected = part if projected is None else projected + part
        up = ahead
    centered, scale = moments(projected)
    xhat = centered * scale
    out_ref[...] = (mixed + (xhat * gain_two + bias_two)).astype(BF).reshape(out_ref.shape)
    ct = ct_ref[...].reshape(size, features).astype(F32)
    gain_two_acc[...] += fold(ct * xhat)
    bias_two_acc[...] += fold(ct)
    e = ct * gain_two
    mean_e = jnp.mean(e, axis=1, keepdims=True)
    mean_ex = jnp.mean(e * xhat, axis=1, keepdims=True)
    gproj = (scale * (e - mean_e - xhat * mean_ex)).astype(BF)

    for cols in pieces:
        g_act = dot(gproj, w_out_ref[cols, :], 1, 1)
        up_low = (g_act * slope_scr[:, cols]).astype(BF)
        up_scr[:, cols] = up_low
        b_in_acc[:, cols] += fold(up_low.astype(F32))
    total = dot(up_scr[...], w_in_ref[...], 1, 1)
    for cols in pieces:
        before = jnp.where(step == 0, 0.0, gw_out_acc[cols, :])
        gw_out_acc[cols, :] = before + dot(act_scr[:, cols], gproj, 0, 0)
        before = jnp.where(step == 0, 0.0, gw_in_acc[:, cols])
        gw_in_acc[:, cols] = before + dot(mixed_low, up_scr[:, cols], 0, 0)
    g_mixed = ct_ref[...].reshape(size, features).astype(F32) + total
    gmixed_ref[...] = g_mixed.reshape(gmixed_ref.shape)
    hid = hidden_ref[...].reshape(size, features).astype(F32)
    cdf, bell = cdf_and_exp(hid)
    centered, scale = moments(hid * cdf)
    yhat = centered * scale
    gain_one_acc[...] += fold(g_mixed * yhat)
    bias_one_acc[...] += fold(g_mixed)
    e = g_mixed * gain_one
    mean_e = jnp.mean(e, axis=1, keepdims=True)
    mean_ey = jnp.mean(e * yhat, axis=1, keepdims=True)
    g_hidden = scale * (e - mean_e - yhat * mean_ey) * (cdf + hid * bell * RSQRT2PI)
    g_low = g_hidden.astype(BF)
    gh_ref[...] = g_low.reshape(gh_ref.shape)
    conv_b_acc[...] += fold(g_low.astype(F32))

    @pl.when(step == steps - 1)
    def _():
        n_wide, n_narrow = blocks
        height, width = hidden_units // n_narrow, features // n_wide
        base = 0 if blocks == (1, 1) else height
        for n in range(n_narrow):
            product = gw_out_acc[n * height : (n + 1) * height, :].astype(BF)
            for w in range(n_wide):
                place_block(
                    gw_out_ref, product[:, w * width : (w + 1) * width], w, n, slice(0, height),
                    blocks,
                )
        copies = []

        def ship(rows):
            for i, ref in enumerate((keep_ref, send_ref)):
                copies.append(
                    pltpu.make_async_copy(
                        gw_ref.at[i, :, rows, :], ref.at[:, rows, :], sems.at[len(copies)]
                    )
                )
                copies[-1].start()

        if blocks != (1, 1):
            ship(pl.ds(0, base))
        row = 0
        for ref in (conv_b_acc, gain_one_acc, bias_one_acc, b_in_acc, gain_two_acc, bias_two_acc):
            summed = jnp.sum(ref[...], axis=0, keepdims=True)
            for j in range(ref.shape[1] // 128):
                sums_ref[row : row + 1, :] = summed[:, j * 128 : (j + 1) * 128]
                row += 1
        sums_ref[row:, :] = jnp.zeros_like(sums_ref[row:, :])
        height, width = features // n_narrow, hidden_units // n_wide
        lanes = gw_in_ref.shape[-1]
        for w in range(n_wide):
            product = gw_in_acc[:, w * width : (w + 1) * width].astype(BF)
            for n in range(n_narrow):
                for j in range(width // lanes):
                    place_block(
                        gw_in_ref,
                        product[n * height : (n + 1) * height, j * lanes : (j + 1) * lanes],
                        w, n, slice(base + j * height, base + (j + 1) * height), blocks,
                    )
        if blocks != (1, 1):
            last = gw_ref.shape[2] - 16
            for i, part in enumerate(in_pair(sums_ref[...])):
                for j in range(4):
                    for side in range(2):
                        gw_ref[side, 4 * i + j, last:, :] = part[16 * j : 16 * (j + 1)]
            ship(pl.ds(base, gw_ref.shape[2] - base))
            for copy in copies:
                copy.wait()


def middle(blocks, hidden, x, ct, w_in, w_out, vec, b_in):
    rows, own, features = x.shape
    hidden_units = w_in.shape[1]
    block_rows = 2
    size = block_rows * own
    total = rows * own
    row_block = pl.BlockSpec((block_rows, own, features), lambda i: (i, 0, 0))
    sums = ((5 * features + hidden_units) // 128 + 63) // 64 * 64
    if blocks == (1, 1):
        dims = [(1, 1, hidden_units, features), (1, 1, features, hidden_units)]
        shapes = [shape(d, BF) for d in dims] + [shape((sums, 128), F32)]
        specs = [whole(v.shape) for v in shapes]
        scratch = []
    else:
        n_wide, n_narrow = blocks
        height = 2 * features * hidden_units // (n_wide * n_narrow * 128) + 16
        shapes = [shape((n_wide * n_narrow // 2, height, 128), BF)] * 2
        specs = [pl.BlockSpec(memory_space=pl.ANY)] * 2
        scratch = [
            pltpu.VMEM((2,) + shapes[0].shape, BF), pltpu.VMEM((sums, 128), F32),
            pltpu.SemaphoreType.DMA((4,)),
        ]
    narrow = pltpu.VMEM((8, features), F32)
    return pl.pallas_call(
        functools.partial(middle_kernel, blocks),
        grid=(rows // block_rows,),
        in_specs=[
            row_block, row_block, row_block, pl.BlockSpec(memory_space=pl.ANY),
            pl.BlockSpec(memory_space=pl.ANY), whole(vec.shape), whole(b_in.shape),
        ],
        out_specs=[row_block, row_block, row_block] + specs,
        out_shape=[shape(x.shape, BF), shape(x.shape, F32), shape(x.shape, BF)] + shapes,
        scratch_shapes=[
            pltpu.VMEM(w_in.shape, BF), pltpu.VMEM(w_out.shape, BF), pltpu.SemaphoreType.DMA((2,)),
            pltpu.VMEM((size, hidden_units), BF), pltpu.VMEM((size, hidden_units), F32),
            pltpu.VMEM((size, hidden_units), BF),
            pltpu.VMEM((hidden_units, features), F32), pltpu.VMEM((features, hidden_units), F32),
            pltpu.VMEM((8, hidden_units), F32), narrow, narrow, narrow, narrow, narrow,
        ] + scratch,
        compiler_params=params(34),
        cost_estimate=cost(2 * total * features * 6 * hidden_units, 34e6),
        name="middle",
    )(hidden, x, ct, w_in, w_out, vec, b_in)


GROUP = 3


def fill_copies(ext, near_hbm, own_hbm, far_hbm, sems):
    rows, own = own_hbm.shape[0], own_hbm.shape[1]
    reach = (ext.shape[1] - own) // 2
    copies = [pltpu.make_async_copy(own_hbm, ext.at[:, pl.ds(reach, own), :], sems.at[0])]
    for i, (halo, side) in enumerate(zip((near_hbm, far_hbm), pair_sides(), strict=True)):
        at = pl.multiple_of(side * (reach + own), reach)
        for r in range(rows):
            source = halo.at[r] if len(halo.shape) == 3 else halo.at[pl.ds(r * reach, reach), :]
            copies.append(
                pltpu.make_async_copy(
                    source, ext.at[r, pl.ds(at, reach), :], sems.at[1 + i * rows + r]
                )
            )
    return copies


def build_masked(lhs, ext, info_ref, tap, forward_masks, first=0):
    rows, extended, features = ext.shape
    taps = info_ref.shape[0] - 1
    reach = STEP * (taps // 2)
    own = extended - 2 * reach
    offset = STEP * tap if forward_masks else STEP * (taps - 1 - tap)
    ids = info_ref[0]
    moved = pltpu.roll(ids, extended - offset, 1)[:, :own]
    used = info_ref[1 + tap]
    if forward_masks:
        used = used[:, reach : reach + own]
    else:
        used = pltpu.roll(used, extended - offset, 1)[:, :own]
    columns = mask_columns((moved == ids[:, reach : reach + own]) & (used == 1))
    at = pl.ds(pl.multiple_of(offset, STEP), own)
    for r in range(rows):
        lhs[r * own : (r + 1) * own, :] = ext[r, at, :] * spread(
            columns[:, first + r : first + r + 1], features
        )


def weight_kernel(blocks, info_ref, gh_ref, x_hbm, near_hbm, far_hbm, *rest):
    if blocks == (1, 1):
        gw_ref, ext, *lhs, fill_sems = rest
    else:
        keep_ref, send_ref, ext, *lhs, fill_sems, gw_ref, sems = rest
    step = pl.program_id(0)
    steps = pl.num_programs(0)
    rows, own, features = gh_ref.shape

    @pl.when(step == 0)
    def _():
        copies = fill_copies(ext, near_hbm, x_hbm, far_hbm, fill_sems)
        for copy in copies:
            copy.start()
        for copy in copies:
            copy.wait()
        build_masked(lhs[0], ext, info_ref, 0, True)

    n_wide, n_narrow = blocks
    height, width = features // n_narrow, features // n_wide
    last_tap = GROUP * steps - 1
    for j in range(GROUP):
        tap = GROUP * step + j
        build_masked(
            lhs[(j + 1) % GROUP], ext, info_ref, jnp.minimum(tap + 1, last_tap), True
        )
        product = dot(lhs[j][...], gh_ref[...].reshape(rows * own, features), 0, 0).astype(BF)
        rows_at = pl.ds(pl.multiple_of(tap * height, height), height)
        for n in range(n_narrow):
            for w in range(n_wide):
                place_block(
                    gw_ref,
                    product[n * height : (n + 1) * height, w * width : (w + 1) * width],
                    w, n, rows_at, blocks,
                )

    if blocks != (1, 1):

        def shipping(at):
            size = GROUP * height
            rows_of = pl.ds(pl.multiple_of(at * size, size), size)
            return [
                pltpu.make_async_copy(
                    gw_ref.at[i, :, rows_of, :], ref.at[:, rows_of, :], sems.at[i]
                )
                for i, ref in enumerate((keep_ref, send_ref))
            ]

        @pl.when(step > 0)
        def _():
            for copy in shipping(step - 1):
                copy.wait()

        for copy in shipping(step):
            copy.start()

        @pl.when(step == steps - 1)
        def _():
            for copy in shipping(step):
                copy.wait()


def weight_gradient(blocks, info, gh, x, near, far, taps):
    rows, own, features = x.shape
    shapes, specs, scratch = gradient_outputs(blocks, taps * features, features)
    return pl.pallas_call(
        functools.partial(weight_kernel, blocks),
        grid=(taps // GROUP,),
        in_specs=[whole(info.shape), whole(gh.shape)] + [pl.BlockSpec(memory_space=pl.ANY)] * 3,
        out_specs=specs,
        out_shape=shapes,
        scratch_shapes=[
            pltpu.VMEM((rows, info.shape[2], features), BF),
            *[pltpu.VMEM((rows * own, features), BF)] * GROUP,
            pltpu.SemaphoreType.DMA((1 + 2 * rows,)),
        ]
        + scratch,
        compiler_params=params(18),
        cost_estimate=cost(2 * rows * own * features * features * taps, 12e6),
        name="weight_gradient",
    )(info, gh, x, near, far)


def input_kernel(
    first, info_ref, w_ref, gh_hbm, near_hbm, far_hbm, gmixed_hbm,
    gx_hbm, ext, *rest,
):
    *lhs, acc, gmixed, fill_sems, in_sem, out_sems = rest
    step = pl.program_id(0)
    steps = pl.num_programs(0)
    rows, own, features = gmixed.shape
    batch = pl.ds(first, rows)
    base = pltpu.make_async_copy(gmixed_hbm.at[batch], gmixed, in_sem)

    @pl.when(step == 0)
    def _():
        copies = fill_copies(
            ext, near_hbm.at[batch], gh_hbm.at[batch], far_hbm.at[batch], fill_sems
        )
        for copy in copies:
            copy.start()
        base.start()
        acc[...] = jnp.zeros_like(acc)
        for copy in copies:
            copy.wait()
        build_masked(lhs[0], ext, info_ref, 0, False, first)

    last_tap = GROUP * steps - 1
    for j in range(GROUP):
        tap = GROUP * step + j
        build_masked(
            lhs[(j + 1) % GROUP], ext, info_ref, jnp.minimum(tap + 1, last_tap), False, first
        )
        acc[...] += dot(lhs[j][...], w_ref[j], 1, 1)

    @pl.when(step == steps - 1)
    def _():
        base.wait()
        copies = []
        for r in range(rows):
            g_in = acc[r * own : (r + 1) * own, :].astype(BF).astype(F32)
            gmixed[r] = gmixed[r] + g_in
            copies.append(pltpu.make_async_copy(gmixed.at[r], gx_hbm.at[first + r], out_sems.at[r]))
            copies[-1].start()
        for copy in copies:
            copy.wait()


def input_gradient(info, conv_w, gh, near, far, gmixed, first, rows):
    _, own, features = gh.shape
    reach = STEP * (conv_w.shape[0] // 2)
    taps = conv_w.shape[0]
    return pl.pallas_call(
        functools.partial(input_kernel, first),
        grid=(taps // GROUP,),
        in_specs=[
            whole(info.shape),
            pl.BlockSpec((GROUP, features, features), lambda i: (i, 0, 0)),
        ]
        + [pl.BlockSpec(memory_space=pl.ANY)] * 4,
        out_specs=pl.BlockSpec(memory_space=pl.ANY),
        out_shape=shape(gmixed.shape, F32),
        input_output_aliases={5: 0},
        scratch_shapes=[
            pltpu.VMEM((rows, own + 2 * reach, features), BF),
            *[pltpu.VMEM((rows * own, features), BF)] * GROUP,
            pltpu.VMEM((rows * own, features), F32),
            pltpu.VMEM((rows, own, features), F32),
            pltpu.SemaphoreType.DMA((1 + 2 * rows,)),
            pltpu.SemaphoreType.DMA,
            pltpu.SemaphoreType.DMA((rows,)),
        ],
        compiler_params=params(10 + rows),
        cost_estimate=cost(2 * rows * own * features * features * taps, 12e6),
        name="input_gradient",
    )(info, conv_w, gh, near, far, gmixed)


class Additions(NamedTuple):
    fn: Any
    operands: tuple
    in_specs: list
    out_specs: list
    out_shape: list
    steps: int


def additions_kernel(fn, count, *refs):
    fn(refs[:count], refs[count:])


def alone(work):
    moved = 3 * sum(v.size for v in work.operands)
    return pl.pallas_call(
        functools.partial(additions_kernel, work.fn, len(work.operands)),
        grid=(work.steps,),
        in_specs=work.in_specs,
        out_specs=work.out_specs,
        out_shape=work.out_shape,
        compiler_params=params(8),
        cost_estimate=cost(moved / 2, moved),
        name="additions",
    )(*work.operands)


def flip(value, axis, bit):
    size = lax.axis_size(axis)
    return lax.ppermute(value, axis, [(i, i ^ bit) for i in range(size)])


def add(a, b):
    return a.astype(F32) + b.astype(F32)


def stepwise(block, axis):
    return pl.BlockSpec(block, lambda i: tuple(i if d == axis else 0 for d in range(len(block))))


def after_core(keep, got, top, extra=0):
    end = keep.shape[1] - extra
    operands = [v.reshape((2, 2, 4) + v.shape[1:]) for v in (keep, got)]

    def fn(ins, outs):
        a_keep, a_send, b_keep, b_send = outs
        keep, got = ins
        for y in range(2):
            for x in range(2):
                total = add(keep[y, x, 0, :end], got[y, x, 0, :end]).astype(BF)
                (a_send if x else a_keep)[y, 0, :top, :] = total[:top]
                (b_send if y else b_keep)[x, 0, :, :] = total[top:]
        if extra:
            total = add(keep[0, 0, 0, end:], keep[0, 1, 0, end:]) + add(
                got[0, 0, 0, end:], got[0, 1, 0, end:]
            )
            for i, part in enumerate(in_pair(total)):
                for ref in (a_keep, a_send):
                    ref[i, 0, top:, :] = part

    dims = [(2, 4, top + extra, 128)] * 2 + [(2, 4, end - top, 128)] * 2
    return Additions(
        fn,
        tuple(operands),
        [stepwise((2, 2, 1) + v.shape[3:], 2) for v in operands],
        [stepwise((2, 1) + d[2:], 1) for d in dims],
        [shape(d, BF) for d in dims],
        4,
    )


def after_first(top, a_keep, a_got, b_keep, b_got):
    extra = a_keep.shape[2] - top

    def fn(ins, outs):
        a_keep, a_got, b_keep, b_got = ins
        a_next, a_send, b_next, b_send = outs
        for keep, got, stay, send in (
            (a_keep, a_got, a_next, a_send),
            (b_keep, b_got, b_next, b_send),
        ):
            n = stay.shape[1] if stay is b_next else top
            stay[0, :n] = add(keep[0, 0, :n], got[0, 0, :n]).astype(BF)
            send[0, :n] = add(keep[1, 0, :n], got[1, 0, :n]).astype(BF)
        if extra:
            total = add(a_keep[0, 0, top:], a_keep[1, 0, top:]) + add(
                a_got[0, 0, top:], a_got[1, 0, top:]
            )
            for i, part in enumerate(in_pair(total)):
                for ref in (a_next, a_send):
                    ref[0, top + i * extra : top + (i + 1) * extra] = part

    dims = [(4, top + 2 * extra, 128)] * 2 + [(4, b_keep.shape[2], 128)] * 2
    operands = (a_keep, a_got, b_keep, b_got)
    return Additions(
        fn,
        operands,
        [stepwise((2, 1) + v.shape[2:], 1) for v in operands],
        [stepwise((1,) + d[1:], 0) for d in dims],
        [shape(d, BF) for d in dims],
        4,
    )


def after_second_kernel(top, a_keep, a_got, b_keep, b_got, *outs):
    extra = (a_keep.shape[1] - top) // 2
    end = top + b_keep.shape[1]
    for i, ref in enumerate(outs):
        ref[:top] = add(a_keep[i, :top], a_got[i, :top]).astype(BF)
        ref[top:end] = add(b_keep[i], b_got[i]).astype(BF)
    if extra:
        for z in range(4):
            high, low = slice(top, top + extra), slice(top + extra, top + 2 * extra)
            total = add(a_keep[z, high], a_keep[z, low]) + add(a_got[z, high], a_got[z, low])
            for i, part in enumerate(in_pair(total)):
                at = end + (4 * i + z) * extra
                for ref in outs:
                    ref[at : at + extra] = part


def after_second(top, a_keep, a_got, b_keep, b_got):
    rows = top + b_keep.shape[1] + 4 * (a_keep.shape[1] - top)
    z = small(
        functools.partial(after_second_kernel, top),
        (a_keep, a_got, b_keep, b_got), [(rows, 128)] * 4,
    )
    return (z[0], *(flip(z[i], "narrow", 2 * i) for i in (1, 2, 3)))


def last_ff_kernel(z0, z1, z2, z3, w_out_ref, w_in_ref, sums_ref):
    out_rows, (height, width) = w_out_ref.shape[0], w_in_ref.shape
    total = add(z0[...], z1[...]) + add(z2[...], z3[...])
    w_out_ref[...] = total[:out_rows]
    for j in range(width // 128):
        at = out_rows + j * height
        w_in_ref[:, 128 * j : 128 * (j + 1)] = total[at : at + height]
    end = out_rows + height * width // 128
    rows = sums_ref.shape[0]
    sums_ref[...] = total[end : end + rows] + total[end + rows :]


def last_conv_kernel(z0, z1, z2, z3, out):
    out[...] = add(z0[...], z1[...]) + add(z2[...], z3[...])


def small(kernel, operands, dims, dtype=BF):
    moved = sum(v.size * v.dtype.itemsize for v in operands) * 2
    return pl.pallas_call(
        kernel,
        out_shape=[shape(d, dtype) for d in dims],
        compiler_params=params(12),
        cost_estimate=cost(moved / 2, moved),
        name="additions",
    )(*operands)


def after(value, *others):
    return lax.optimization_barrier((value, others))[0]


def body(
    inputs, conv_w, conv_b, ln1_gain, ln1_bias, w_in, b_in, w_out, ln2_gain, ln2_bias,
    segments, tap_mask, cotangent,
):
    rows, own, features = inputs.shape
    taps = conv_w.shape[0]
    reach = STEP * (taps // 2)
    hidden_units = w_in.shape[1]
    n_wide, n_narrow = lax.axis_size("wide"), lax.axis_size("narrow")
    by_hand = (n_wide, n_narrow) == (4, 8)
    blocks = (4, 8) if by_hand else (1, 1)

    near_pairs = [(i, i ^ 1) for i in range(n_wide)]
    far_pairs = [(i, i + 1 if i % 2 else i - 1) for i in range(1, n_wide - 1)]

    def exchange(near, far):
        far = lax.ppermute(far, "wide", far_pairs)
        return lax.ppermute(near, "wide", near_pairs), far

    def halos(value):
        ends = [
            lax.dynamic_slice_in_dim(value, side * (own - reach), reach, axis=1)
            for side in pair_sides()
        ]
        return exchange(*ends)

    in_place = functools.partial(pltpu.with_memory_space_constraint, memory_space=pltpu.HBM)
    *ends, info = pack(
        in_place(inputs), in_place(segments), in_place(jnp.transpose(tap_mask, (1, 0, 2))), reach
    )
    x_near, x_far = exchange(*ends)
    vec = jnp.stack([conv_b, ln1_gain, ln1_bias, ln2_gain, ln2_bias]).astype(F32)
    vec = jnp.pad(vec, ((0, 3), (0, 0)))

    acc = conv_inner(info, in_place(inputs), in_place(conv_w))
    hidden, info = conv_outer(info, acc, x_near, x_far, conv_w, vec)
    out, gmixed, gh, *grads = middle(
        blocks, hidden, inputs, cotangent, w_in, w_out, vec, b_in.astype(F32)[None]
    )
    if not by_hand:
        gh_near, gh_far = halos(gh)
        gconv = weight_gradient(blocks, info, gh, inputs, x_near, x_far, taps)
        gx = input_gradient(info, conv_w, gh, gh_near, gh_far, gmixed, 0, rows)

        def reduce(value, dims, wide_dim, narrow_dim):
            value = lax.psum_scatter(
                value.reshape(dims), "narrow", scatter_dimension=narrow_dim, tiled=True
            )
            return lax.psum_scatter(value, "wide", scatter_dimension=wide_dim, tiled=True).astype(
                F32
            )

        grad_w_out = reduce(grads[0], (hidden_units, features), 1, 0)
        grad_w_in = reduce(grads[1], (features, hidden_units), 1, 0)
        grad_conv = reduce(gconv[0], (taps, features, features), 2, 1)
        sums = lax.psum(grads[2], ("wide", "narrow"))
    else:
        together = lax.optimization_barrier
        cuts = (0, (3 * rows + 4) // 8, rows - rows // 4, rows)

        def inputs_part(i, gx):
            first, end = cuts[i], cuts[i + 1]
            return input_gradient(info, conv_w, gh, gh_near, gh_far, gx, first, end - first)

        height = features // n_narrow
        f_top = (grads[0].shape[1] - 16) * 3 // 4 // 16 * 16
        c_top = taps * height // 2 // 16 * 16
        f_got = flip(grads[1], "wide", 1)
        gh_near, gh_far = halos(gh)
        f = alone(after_core(grads[0], f_got, f_top, 16))
        f_got = flip(f[1], "narrow", 1), flip(f[3], "wide", 2)
        c = weight_gradient(blocks, info, after(gh, *f), inputs, x_near, x_far, taps)

        c, f, f_got, gh_near, gh_far = together((c, f, f_got, gh_near, gh_far))
        c_got = flip(c[1], "wide", 1)
        f = alone(after_first(f_top, f[0], f_got[0], f[2], f_got[1]))
        f_got = flip(f[1], "wide", 2), flip(f[3], "narrow", 1)
        gx = inputs_part(0, after(gmixed, *f))

        gx, c, c_got, f, f_got = together((gx, c[0], c_got, f, f_got))
        c = alone(after_core(c, c_got, c_top))
        c_got = flip(c[1], "narrow", 1), flip(c[3], "wide", 2)
        f = after_second(f_top, *after((f[0], f_got[0], f[2], f_got[1]), *c))
        gx = inputs_part(1, after(gx, *c, f[0]))

        gx, c, c_got, f = together((gx, c, c_got, f))
        c = alone(after_first(c_top, c[0], c_got[0], c[2], c_got[1]))
        c_got = flip(c[1], "wide", 2), flip(c[3], "narrow", 1)
        gx = inputs_part(2, after(gx, *c))

        gx, c, c_got, f = together((gx, c, c_got, f))
        c = after_second(c_top, c[0], c_got[0], c[2], c_got[1])
        f = after(f, c[0])
        grad_w_out, grad_w_in, sums = small(
            last_ff_kernel, f,
            [(hidden_units // n_narrow, 128), (height, hidden_units // n_wide), (64, 128)],
            F32,
        )
        grad_conv = small(last_conv_kernel, c, [(taps * height, 128)], F32)[0]
        grad_conv = grad_conv.reshape(taps, height, features // n_wide)
    sums = sums.reshape(-1)
    starts = [0, features, 2 * features, 3 * features]
    starts += [starts[-1] + hidden_units, starts[-1] + hidden_units + features]
    sizes = [features, features, features, hidden_units, features, features]
    vectors = [sums[a : a + n] for a, n in zip(starts, sizes, strict=True)]
    return (
        out, gx, grad_conv, vectors[0], vectors[1], vectors[2], grad_w_in, vectors[3],
        grad_w_out, vectors[4], vectors[5],
    )


def solution(mesh):
    split = P("narrow", "wide", None)
    placed = (split,) + (P(),) * 9 + (P("narrow", "wide"), P("narrow", None, "wide"), split)
    return jax.shard_map(
        body,
        mesh=mesh,
        in_specs=placed,
        out_specs=(
            split, split, P(None, "narrow", "wide"), P(), P(), P(), P("narrow", "wide"), P(),
            P("narrow", "wide"), P(), P(),
        ),
        check_vma=False,
    )
```

```python
import functools
from typing import Any, NamedTuple

import jax
import jax.numpy as jnp
from jax import lax
from jax.experimental import pallas as pl
from jax.experimental.pallas import tpu as pltpu
from jax.sharding import PartitionSpec as P

STEP = 32
BF = jnp.bfloat16
F32 = jnp.float32
RSQRT2 = 0.7071067811865476
RSQRT2PI = 0.3989422804014327
EPS = 1e-05


def params(mebibytes):
    return pltpu.CompilerParams(vmem_limit_bytes=mebibytes * 1024 * 1024)


def cost(flops, moved):
    return pl.CostEstimate(
        flops=int(flops / 50), bytes_accessed=int(moved / 50), transcendentals=0
    )


def whole(shape):
    rank = len(shape)
    return pl.BlockSpec(shape, lambda *_: (0,) * rank, pipeline_mode=pl.Buffered(1))


def shape(dims, dtype):
    return jax.ShapeDtypeStruct(dims, dtype)


def mask_columns(matched):
    return jnp.where(matched, 1.0, 0.0).astype(F32).T


def spread(column, width):
    wide = jnp.broadcast_to(column, (column.shape[0], 128)).astype(BF)
    return jnp.concatenate([wide] * (width // 128), axis=1)


def dot(left, right, left_dim, right_dim):
    return lax.dot_general(
        left, right, (((left_dim,), (right_dim,)), ((), ())), preferred_element_type=F32
    )


def cdf_and_exp(values):
    return 0.5 + 0.5 * lax.erf(values * RSQRT2), jnp.exp(-0.5 * values * values)


def in_pair(value):
    high = value.astype(BF)
    return high, (value - high.astype(F32)).astype(BF)


def fold(values):
    return values.reshape(-1, 8, values.shape[-1]).sum(0)


def pair_sides():
    odd = lax.axis_index("wide") % 2
    return 1 - odd, odd


PACK_ROWS = 32


def pack_kernel(
    x_hbm, ids_hbm, used_hbm, near_ref, far_ref, info_ref, ids, sems, info_sems
):
    rows, own, features = x_hbm.shape
    count = info_ref.shape[0]
    reach = (near_ref.shape[0] - PACK_ROWS) // rows
    near, far = pair_sides()
    ends = tuple(
        (ref, pl.multiple_of(side * (own - reach), reach)) for ref, side in ((near_ref, near), (far_ref, far))
    )
    loads = [
        pltpu.make_async_copy(ids_hbm, ids, info_sems.at[0]),
        pltpu.make_async_copy(used_hbm, info_ref.at[pl.ds(1, count - 1)], info_sems.at[1]),
    ]
    for load in loads:
        load.start()
    copies = []
    for side, (out, start) in enumerate(ends):
        for r in range(rows):
            copies.append(
                pltpu.make_async_copy(
                    x_hbm.at[r, pl.ds(start, reach), :],
                    out.at[pl.ds(r * reach, reach), :],
                    sems.at[side * rows + r],
                )
            )
            copies[-1].start()
    for load in loads:
        load.wait()
    info_ref[0] = ids[...] + 1
    for side, (out, start) in enumerate(ends):
        lines = []
        for q in range(PACK_ROWS // rows):
            group = [
                info_ref[k, :, pl.ds(start, reach)].astype(F32)
                if k < count
                else jnp.zeros((rows, reach), F32)
                for k in range(q * features // reach, (q + 1) * features // reach)
            ]
            lines.append(jnp.concatenate(group, axis=1))
        out[rows * reach :, :] = jnp.concatenate(lines, axis=0).astype(BF)
    for copy in copies:
        copy.wait()


def pack(x, ids, used, reach):
    rows, own, features = x.shape
    packed = shape((rows * reach + PACK_ROWS, features), BF)
    return pl.pallas_call(
        pack_kernel,
        grid=(1,),
        in_specs=[pl.BlockSpec(memory_space=pltpu.HBM)] * 3,
        out_specs=[whole(packed.shape)] * 2 + [whole((1 + used.shape[0], rows, own))],
        out_shape=[packed, packed, shape((1 + used.shape[0], rows, own), jnp.int32)],
        scratch_shapes=[
            pltpu.VMEM(ids.shape, jnp.int32),
            pltpu.SemaphoreType.DMA((2 * rows,)),
            pltpu.SemaphoreType.DMA((2,)),
        ],
        compiler_params=params(6),
        cost_estimate=cost(1e6, 4e6),
        name="pack",
    )(x, ids, used)


def put_masked(lhs, sources, columns, n, features):
    for r, source in enumerate(sources):
        lhs[r * n : (r + 1) * n, :] = source * spread(columns[:, r : r + 1], features)


def conv_inner_kernel(info_ref, x_ref, w_ref, acc_ref, even, odd):
    step = pl.program_id(0)
    rows, own, features = x_ref.shape
    taps = info_ref.shape[0] - 1
    half = taps // 2
    order = [half] + [k for k in range(taps) if k != half]
    buffers = (even, odd)

    def span(k):
        shift = STEP * (k - half)
        return max(0, -shift), own - max(0, shift), shift

    def build(i):
        k = order[i]
        low, high, shift = span(k)
        ids = info_ref[0]
        matched = (ids[:, low + shift : high + shift] == ids[:, low:high]) & (
            info_ref[1 + k][:, low:high] == 1
        )
        put_masked(
            buffers[i % 2],
            [x_ref[r, low + shift : high + shift, :] for r in range(rows)],
            mask_columns(matched), high - low, features,
        )

    def run(i):
        low, high, _ = span(order[i])
        n = high - low
        if i + 1 < taps:
            build(i + 1)
        product = dot(buffers[i % 2][: rows * n, :], w_ref[0], 1, 0).reshape(rows, n, features)
        if i == 0:
            acc_ref[...] = product
        else:
            acc_ref[:, low:high, :] += product

    pl.when(step == 0)(functools.partial(build, 0))
    for i in range(taps):
        pl.when(step == i)(functools.partial(run, i))


def conv_inner(info, x, conv_w):
    rows, own, features = x.shape
    taps = conv_w.shape[0]
    half = taps // 2

    def tap_of(i):
        return jnp.where(i == 0, half, jnp.where(i <= half, i - 1, i))

    return pl.pallas_call(
        conv_inner_kernel,
        grid=(taps,),
        in_specs=[
            whole(info.shape),
            whole(x.shape),
            pl.BlockSpec((1, features, features), lambda i: (tap_of(i), 0, 0)),
        ],
        out_specs=whole(x.shape),
        out_shape=shape(x.shape, F32),
        scratch_shapes=[pltpu.VMEM((rows * own, features), BF)] * 2,
        compiler_params=params(12),
        cost_estimate=cost(2 * rows * own * features * features * taps * 0.72, 11e6),
        name="conv_inner",
    )(info, x, conv_w)


def conv_outer_kernel(
    own_info_ref, near_hbm, far_hbm, low_w_ref, high_w_ref, vec_ref, acc_hbm,
    hidden_ref, info_ref, acc, *rest,
):
    even, odd, (halos, sem, halo_sems) = rest[:2], rest[2:4], rest[4:]
    step = pl.program_id(0)
    rows, own, features = hidden_ref.shape
    taps = info_ref.shape[0] - 1
    half = taps // 2
    reach = STEP * half
    buffers = ((even[0], even[1]), (odd[0], odd[1]))
    load = pltpu.make_async_copy(acc_hbm, acc, sem)

    def span(k):
        n = STEP * abs(k - half)
        return (0 if k < half else own - n), n

    def sides(i):
        return (i, low_w_ref, 0), (taps - 1 - i, high_w_ref, 1)

    def build(i):
        for k, _, side in sides(i):
            low, n = span(k)
            source = 0 if side else reach - n
            at = reach + low
            shift = n if side else -n
            ids = info_ref[0]
            matched = (info_ref[1 + k][:, at : at + n] == 1) & (
                ids[:, at + shift : at + shift + n] == ids[:, at : at + n]
            )
            put_masked(
                buffers[i % 2][side],
                [halos[side, r * reach + source : r * reach + source + n, :] for r in range(rows)],
                mask_columns(matched), n, features,
            )

    def run(i):
        if i + 1 < half:
            build(i + 1)
        for k, w_ref, side in sides(i):
            low, n = span(k)
            product = dot(buffers[i % 2][side][: rows * n, :], w_ref[0], 1, 0)
            acc[:, low : low + n, :] += product.reshape(rows, n, features)

    @pl.when(step == 0)
    def _():
        copies = [
            pltpu.make_async_copy(src, halos.at[side], halo_sems.at[i])
            for i, (src, side) in enumerate(zip((near_hbm, far_hbm), pair_sides(), strict=True))
        ]
        for copy in copies:
            copy.start()
        load.start()
        for copy in copies:
            copy.wait()
        for side, at in enumerate((0, reach + own)):
            lines = halos[side, rows * reach :, :].astype(F32)
            for k in range(taps + 1):
                q, m = divmod(k, features // reach)
                part = lines[q * rows : (q + 1) * rows, m * reach : (m + 1) * reach]
                info_ref[k, :, at : at + reach] = part.astype(jnp.int32)
        info_ref[:, :, reach : reach + own] = own_info_ref[...]
        build(0)
        load.wait()

    for i in range(half):
        pl.when(step == i)(functools.partial(run, i))

    @pl.when(step == half - 1)
    def _():
        hidden_ref[...] = (acc[...] + vec_ref[0:1, :]).astype(BF)


def conv_outer(info, acc, near, far, conv_w, vec):
    rows, own, features = acc.shape
    taps = conv_w.shape[0]
    half = taps // 2
    reach = STEP * half
    info_dims = (1 + taps, rows, own + 2 * reach)
    return pl.pallas_call(
        conv_outer_kernel,
        grid=(half,),
        in_specs=[
            whole(info.shape),
            pl.BlockSpec(memory_space=pl.ANY),
            pl.BlockSpec(memory_space=pl.ANY),
            pl.BlockSpec((1, features, features), lambda i: (i, 0, 0)),
            pl.BlockSpec((1, features, features), lambda i: (taps - 1 - i, 0, 0)),
            whole(vec.shape),
            pl.BlockSpec(memory_space=pl.ANY),
        ],
        out_specs=[whole(acc.shape), whole(info_dims)],
        out_shape=[shape(acc.shape, BF), shape(info_dims, jnp.int32)],
        scratch_shapes=[pltpu.VMEM(acc.shape, F32)]
        + [pltpu.VMEM((rows * reach, features), BF)] * 4
        + [
            pltpu.VMEM((2,) + near.shape, BF),
            pltpu.SemaphoreType.DMA,
            pltpu.SemaphoreType.DMA((2,)),
        ],
        compiler_params=params(14),
        cost_estimate=cost(2 * rows * own * features * features * taps * 0.28, 11e6),
        name="conv_outer",
    )(info, near, far, conv_w, conv_w, vec, acc)


def place_block(out_ref, value, dest_wide, dest_narrow, rows_at, blocks):
    if blocks == (1, 1):
        out_ref[0, 0, rows_at, :] = value
        return
    rel_wide = lax.axis_index("wide") ^ dest_wide
    rel_narrow = lax.axis_index("narrow") ^ dest_narrow
    index = (rel_wide >> 1) * 8 + (rel_narrow & 1) * 4 + (rel_narrow >> 1)
    out_ref[rel_wide & 1, index, rows_at, :] = value


def gradient_outputs(blocks, height, width):
    if blocks == (1, 1):
        dims = (1, 1, height, width)
        return [shape(dims, BF)], [whole(dims)], []
    n_wide, n_narrow = blocks
    height, width = height // n_narrow, width // n_wide
    dims = (n_wide * n_narrow // 2, height, width)
    return (
        [shape(dims, BF)] * 2,
        [pl.BlockSpec(memory_space=pl.ANY)] * 2,
        [pltpu.VMEM((2,) + dims, BF), pltpu.SemaphoreType.DMA((2,))],
    )


def moments(values):
    centered = values - jnp.mean(values, axis=1, keepdims=True)
    return centered, lax.rsqrt(jnp.mean(centered * centered, axis=1, keepdims=True) + EPS)


def middle_kernel(
    blocks,
    hidden_ref, x_ref, ct_ref, w_in_hbm, w_out_hbm, vec_ref, b_in_ref,
    out_ref, gmixed_ref, gh_ref, *rest,
):
    if blocks == (1, 1):
        gw_out_ref, gw_in_ref, sums_ref, *rest = rest
    else:
        keep_ref, send_ref, *rest = rest
    (
        w_in_ref, w_out_ref, load_sems, act_scr, slope_scr, up_scr, gw_out_acc, gw_in_acc, b_in_acc, gain_one_acc,
        bias_one_acc, gain_two_acc, bias_two_acc, conv_b_acc, *rest,
    ) = rest
    if blocks != (1, 1):
        gw_ref, sums_ref, sems = rest
        gw_out_ref = gw_in_ref = gw_ref
    step = pl.program_id(0)
    steps = pl.num_programs(0)
    size = act_scr.shape[0]
    features, hidden_units = w_in_ref.shape
    loads = [
        pltpu.make_async_copy(src, dst, load_sems.at[i])
        for i, (src, dst) in enumerate(((w_in_hbm, w_in_ref), (w_out_hbm, w_out_ref)))
    ]

    @pl.when(step == 0)
    def _():
        for load in loads:
            load.start()
        for ref in (
            b_in_acc, gain_one_acc, bias_one_acc, gain_two_acc, bias_two_acc, conv_b_acc,
        ):
            ref[...] = jnp.zeros_like(ref)
        for load in loads:
            load.wait()

    gain_one = vec_ref[1:2, :]
    bias_one = vec_ref[2:3, :]
    gain_two = vec_ref[3:4, :]
    bias_two = vec_ref[4:5, :]
    chunk = 512
    count = hidden_units // chunk
    pieces = [slice(j * chunk, (j + 1) * chunk) for j in range(count)]

    hid = hidden_ref[...].reshape(size, features).astype(F32)
    centered, scale = moments(hid * (0.5 + 0.5 * lax.erf(hid * RSQRT2)))
    mixed = x_ref[...].reshape(size, features).astype(F32) + (
        centered * scale * gain_one + bias_one
    )
    mixed_low = mixed.astype(BF)

    def up_part(cols):
        return dot(mixed_low, w_in_ref[:, cols], 1, 0) + b_in_ref[:, cols]

    projected = None
    up = up_part(pieces[0])
    for j, cols in enumerate(pieces):
        ahead = up_part(pieces[j + 1]) if j + 1 < count else None
        cdf, bell = cdf_and_exp(up)
        act_low = (up * cdf).astype(BF)
        slope_scr[:, cols] = cdf + up * bell * RSQRT2PI
        act_scr[:, cols] = act_low
        part = dot(act_low, w_out_ref[cols, :], 1, 0)
        projected = part if projected is None else projected + part
        up = ahead
    centered, scale = moments(projected)
    xhat = centered * scale
    out_ref[...] = (mixed + (xhat * gain_two + bias_two)).astype(BF).reshape(out_ref.shape)
    ct = ct_ref[...].reshape(size, features).astype(F32)
    gain_two_acc[...] += fold(ct * xhat)
    bias_two_acc[...] += fold(ct)
    e = ct * gain_two
    mean_e = jnp.mean(e, axis=1, keepdims=True)
    mean_ex = jnp.mean(e * xhat, axis=1, keepdims=True)
    gproj = (scale * (e - mean_e - xhat * mean_ex)).astype(BF)

    for cols in pieces:
        g_act = dot(gproj, w_out_ref[cols, :], 1, 1)
        up_low = (g_act * slope_scr[:, cols]).astype(BF)
        up_scr[:, cols] = up_low
        b_in_acc[:, cols] += fold(up_low.astype(F32))
    total = dot(up_scr[...], w_in_ref[...], 1, 1)
    for cols in pieces:
        before = jnp.where(step == 0, 0.0, gw_out_acc[cols, :])
        gw_out_acc[cols, :] = before + dot(act_scr[:, cols], gproj, 0, 0)
        before = jnp.where(step == 0, 0.0, gw_in_acc[:, cols])
        gw_in_acc[:, cols] = before + dot(mixed_low, up_scr[:, cols], 0, 0)
    g_mixed = ct_ref[...].reshape(size, features).astype(F32) + total
    gmixed_ref[...] = g_mixed.reshape(gmixed_ref.shape)
    hid = hidden_ref[...].reshape(size, features).astype(F32)
    cdf, bell = cdf_and_exp(hid)
    centered, scale = moments(hid * cdf)
    yhat = centered * scale
    gain_one_acc[...] += fold(g_mixed * yhat)
    bias_one_acc[...] += fold(g_mixed)
    e = g_mixed * gain_one
    mean_e = jnp.mean(e, axis=1, keepdims=True)
    mean_ey = jnp.mean(e * yhat, axis=1, keepdims=True)
    g_hidden = scale * (e - mean_e - yhat * mean_ey) * (cdf + hid * bell * RSQRT2PI)
    g_low = g_hidden.astype(BF)
    gh_ref[...] = g_low.reshape(gh_ref.shape)
    conv_b_acc[...] += fold(g_low.astype(F32))

    @pl.when(step == steps - 1)
    def _():
        n_wide, n_narrow = blocks
        height, width = hidden_units // n_narrow, features // n_wide
        base = 0 if blocks == (1, 1) else height
        for n in range(n_narrow):
            product = gw_out_acc[n * height : (n + 1) * height, :].astype(BF)
            for w in range(n_wide):
                place_block(
                    gw_out_ref, product[:, w * width : (w + 1) * width], w, n, slice(0, height),
                    blocks,
                )
        copies = []

        def ship(rows):
            for i, ref in enumerate((keep_ref, send_ref)):
                copies.append(
                    pltpu.make_async_copy(
                        gw_ref.at[i, :, rows, :], ref.at[:, rows, :], sems.at[len(copies)]
                    )
                )
                copies[-1].start()

        if blocks != (1, 1):
            ship(pl.ds(0, base))
        row = 0
        for ref in (conv_b_acc, gain_one_acc, bias_one_acc, b_in_acc, gain_two_acc, bias_two_acc):
            summed = jnp.sum(ref[...], axis=0, keepdims=True)
            for j in range(ref.shape[1] // 128):
                sums_ref[row : row + 1, :] = summed[:, j * 128 : (j + 1) * 128]
                row += 1
        sums_ref[row:, :] = jnp.zeros_like(sums_ref[row:, :])
        height, width = features // n_narrow, hidden_units // n_wide
        lanes = gw_in_ref.shape[-1]
        for w in range(n_wide):
            product = gw_in_acc[:, w * width : (w + 1) * width].astype(BF)
            for n in range(n_narrow):
                for j in range(width // lanes):
                    place_block(
                        gw_in_ref,
                        product[n * height : (n + 1) * height, j * lanes : (j + 1) * lanes],
                        w, n, slice(base + j * height, base + (j + 1) * height), blocks,
                    )
        if blocks != (1, 1):
            last = gw_ref.shape[2] - 16
            for i, part in enumerate(in_pair(sums_ref[...])):
                for j in range(4):
                    for side in range(2):
                        gw_ref[side, 4 * i + j, last:, :] = part[16 * j : 16 * (j + 1)]
            ship(pl.ds(base, gw_ref.shape[2] - base))
            for copy in copies:
                copy.wait()


def middle(blocks, hidden, x, ct, w_in, w_out, vec, b_in):
    rows, own, features = x.shape
    hidden_units = w_in.shape[1]
    block_rows = 2
    size = block_rows * own
    total = rows * own
    row_block = pl.BlockSpec((block_rows, own, features), lambda i: (i, 0, 0))
    sums = ((5 * features + hidden_units) // 128 + 63) // 64 * 64
    if blocks == (1, 1):
        dims = [(1, 1, hidden_units, features), (1, 1, features, hidden_units)]
        shapes = [shape(d, BF) for d in dims] + [shape((sums, 128), F32)]
        specs = [whole(v.shape) for v in shapes]
        scratch = []
    else:
        n_wide, n_narrow = blocks
        height = 2 * features * hidden_units // (n_wide * n_narrow * 128) + 16
        shapes = [shape((n_wide * n_narrow // 2, height, 128), BF)] * 2
        specs = [pl.BlockSpec(memory_space=pl.ANY)] * 2
        scratch = [
            pltpu.VMEM((2,) + shapes[0].shape, BF), pltpu.VMEM((sums, 128), F32),
            pltpu.SemaphoreType.DMA((4,)),
        ]
    narrow = pltpu.VMEM((8, features), F32)
    return pl.pallas_call(
        functools.partial(middle_kernel, blocks),
        grid=(rows // block_rows,),
        in_specs=[
            row_block, row_block, row_block, pl.BlockSpec(memory_space=pl.ANY),
            pl.BlockSpec(memory_space=pl.ANY), whole(vec.shape), whole(b_in.shape),
        ],
        out_specs=[row_block, row_block, row_block] + specs,
        out_shape=[shape(x.shape, BF), shape(x.shape, F32), shape(x.shape, BF)] + shapes,
        scratch_shapes=[
            pltpu.VMEM(w_in.shape, BF), pltpu.VMEM(w_out.shape, BF), pltpu.SemaphoreType.DMA((2,)),
            pltpu.VMEM((size, hidden_units), BF), pltpu.VMEM((size, hidden_units), F32),
            pltpu.VMEM((size, hidden_units), BF),
            pltpu.VMEM((hidden_units, features), F32), pltpu.VMEM((features, hidden_units), F32),
            pltpu.VMEM((8, hidden_units), F32), narrow, narrow, narrow, narrow, narrow,
        ] + scratch,
        compiler_params=params(34),
        cost_estimate=cost(2 * total * features * 6 * hidden_units, 34e6),
        name="middle",
    )(hidden, x, ct, w_in, w_out, vec, b_in)


GROUP = 3


def fill_copies(ext, near_hbm, own_hbm, far_hbm, sems):
    rows, own = own_hbm.shape[0], own_hbm.shape[1]
    reach = (ext.shape[1] - own) // 2
    copies = [pltpu.make_async_copy(own_hbm, ext.at[:, pl.ds(reach, own), :], sems.at[0])]
    for i, (halo, side) in enumerate(zip((near_hbm, far_hbm), pair_sides(), strict=True)):
        at = pl.multiple_of(side * (reach + own), reach)
        for r in range(rows):
            source = halo.at[r] if len(halo.shape) == 3 else halo.at[pl.ds(r * reach, reach), :]
            copies.append(
                pltpu.make_async_copy(
                    source, ext.at[r, pl.ds(at, reach), :], sems.at[1 + i * rows + r]
                )
            )
    return copies


def build_masked(lhs, ext, info_ref, tap, forward_masks, first=0):
    rows, extended, features = ext.shape
    taps = info_ref.shape[0] - 1
    reach = STEP * (taps // 2)
    own = extended - 2 * reach
    offset = STEP * tap if forward_masks else STEP * (taps - 1 - tap)
    ids = info_ref[0]
    moved = pltpu.roll(ids, extended - offset, 1)[:, :own]
    used = info_ref[1 + tap]
    if forward_masks:
        used = used[:, reach : reach + own]
    else:
        used = pltpu.roll(used, extended - offset, 1)[:, :own]
    columns = mask_columns((moved == ids[:, reach : reach + own]) & (used == 1))
    at = pl.ds(pl.multiple_of(offset, STEP), own)
    for r in range(rows):
        lhs[r * own : (r + 1) * own, :] = ext[r, at, :] * spread(
            columns[:, first + r : first + r + 1], features
        )


def weight_kernel(blocks, info_ref, gh_ref, x_hbm, near_hbm, far_hbm, *rest):
    if blocks == (1, 1):
        gw_ref, ext, *lhs, fill_sems = rest
    else:
        keep_ref, send_ref, ext, *lhs, fill_sems, gw_ref, sems = rest
    step = pl.program_id(0)
    steps = pl.num_programs(0)
    rows, own, features = gh_ref.shape

    @pl.when(step == 0)
    def _():
        copies = fill_copies(ext, near_hbm, x_hbm, far_hbm, fill_sems)
        for copy in copies:
            copy.start()
        for copy in copies:
            copy.wait()
        build_masked(lhs[0], ext, info_ref, 0, True)

    n_wide, n_narrow = blocks
    height, width = features // n_narrow, features // n_wide
    last_tap = GROUP * steps - 1
    for j in range(GROUP):
        tap = GROUP * step + j
        build_masked(
            lhs[(j + 1) % GROUP], ext, info_ref, jnp.minimum(tap + 1, last_tap), True
        )
        product = dot(lhs[j][...], gh_ref[...].reshape(rows * own, features), 0, 0).astype(BF)
        rows_at = pl.ds(pl.multiple_of(tap * height, height), height)
        for n in range(n_narrow):
            for w in range(n_wide):
                place_block(
                    gw_ref,
                    product[n * height : (n + 1) * height, w * width : (w + 1) * width],
                    w, n, rows_at, blocks,
                )

    if blocks != (1, 1):

        def shipping(at):
            size = GROUP * height
            rows_of = pl.ds(pl.multiple_of(at * size, size), size)
            return [
                pltpu.make_async_copy(
                    gw_ref.at[i, :, rows_of, :], ref.at[:, rows_of, :], sems.at[i]
                )
                for i, ref in enumerate((keep_ref, send_ref))
            ]

        @pl.when(step > 0)
        def _():
            for copy in shipping(step - 1):
                copy.wait()

        for copy in shipping(step):
            copy.start()

        @pl.when(step == steps - 1)
        def _():
            for copy in shipping(step):
                copy.wait()


def weight_gradient(blocks, info, gh, x, near, far, taps):
    rows, own, features = x.shape
    shapes, specs, scratch = gradient_outputs(blocks, taps * features, features)
    return pl.pallas_call(
        functools.partial(weight_kernel, blocks),
        grid=(taps // GROUP,),
        in_specs=[whole(info.shape), whole(gh.shape)] + [pl.BlockSpec(memory_space=pl.ANY)] * 3,
        out_specs=specs,
        out_shape=shapes,
        scratch_shapes=[
            pltpu.VMEM((rows, info.shape[2], features), BF),
            *[pltpu.VMEM((rows * own, features), BF)] * GROUP,
            pltpu.SemaphoreType.DMA((1 + 2 * rows,)),
        ]
        + scratch,
        compiler_params=params(18),
        cost_estimate=cost(2 * rows * own * features * features * taps, 12e6),
        name="weight_gradient",
    )(info, gh, x, near, far)


def input_kernel(
    first, info_ref, w_ref, gh_hbm, near_hbm, far_hbm, gmixed_hbm,
    gx_hbm, ext, *rest,
):
    *lhs, acc, gmixed, fill_sems, in_sem, out_sems = rest
    step = pl.program_id(0)
    steps = pl.num_programs(0)
    rows, own, features = gmixed.shape
    batch = pl.ds(first, rows)
    base = pltpu.make_async_copy(gmixed_hbm.at[batch], gmixed, in_sem)

    @pl.when(step == 0)
    def _():
        copies = fill_copies(
            ext, near_hbm.at[batch], gh_hbm.at[batch], far_hbm.at[batch], fill_sems
        )
        for copy in copies:
            copy.start()
        base.start()
        acc[...] = jnp.zeros_like(acc)
        for copy in copies:
            copy.wait()
        build_masked(lhs[0], ext, info_ref, 0, False, first)

    last_tap = GROUP * steps - 1
    for j in range(GROUP):
        tap = GROUP * step + j
        build_masked(
            lhs[(j + 1) % GROUP], ext, info_ref, jnp.minimum(tap + 1, last_tap), False, first
        )
        acc[...] += dot(lhs[j][...], w_ref[j], 1, 1)

    @pl.when(step == steps - 1)
    def _():
        base.wait()
        copies = []
        for r in range(rows):
            g_in = acc[r * own : (r + 1) * own, :].astype(BF).astype(F32)
            gmixed[r] = gmixed[r] + g_in
            copies.append(pltpu.make_async_copy(gmixed.at[r], gx_hbm.at[first + r], out_sems.at[r]))
            copies[-1].start()
        for copy in copies:
            copy.wait()


def input_gradient(info, conv_w, gh, near, far, gmixed, first, rows):
    _, own, features = gh.shape
    reach = STEP * (conv_w.shape[0] // 2)
    taps = conv_w.shape[0]
    return pl.pallas_call(
        functools.partial(input_kernel, first),
        grid=(taps // GROUP,),
        in_specs=[
            whole(info.shape),
            pl.BlockSpec((GROUP, features, features), lambda i: (i, 0, 0)),
        ]
        + [pl.BlockSpec(memory_space=pl.ANY)] * 4,
        out_specs=pl.BlockSpec(memory_space=pl.ANY),
        out_shape=shape(gmixed.shape, F32),
        input_output_aliases={5: 0},
        scratch_shapes=[
            pltpu.VMEM((rows, own + 2 * reach, features), BF),
            *[pltpu.VMEM((rows * own, features), BF)] * GROUP,
            pltpu.VMEM((rows * own, features), F32),
            pltpu.VMEM((rows, own, features), F32),
            pltpu.SemaphoreType.DMA((1 + 2 * rows,)),
            pltpu.SemaphoreType.DMA,
            pltpu.SemaphoreType.DMA((rows,)),
        ],
        compiler_params=params(10 + rows),
        cost_estimate=cost(2 * rows * own * features * features * taps, 12e6),
        name="input_gradient",
    )(info, conv_w, gh, near, far, gmixed)


class Additions(NamedTuple):
    fn: Any
    operands: tuple
    in_specs: list
    out_specs: list
    out_shape: list
    steps: int


def additions_kernel(fn, count, *refs):
    fn(refs[:count], refs[count:])


def alone(work):
    moved = 3 * sum(v.size for v in work.operands)
    return pl.pallas_call(
        functools.partial(additions_kernel, work.fn, len(work.operands)),
        grid=(work.steps,),
        in_specs=work.in_specs,
        out_specs=work.out_specs,
        out_shape=work.out_shape,
        compiler_params=params(8),
        cost_estimate=cost(moved / 2, moved),
        name="additions",
    )(*work.operands)


def flip(value, axis, bit):
    size = lax.axis_size(axis)
    return lax.ppermute(value, axis, [(i, i ^ bit) for i in range(size)])


def add(a, b):
    return a.astype(F32) + b.astype(F32)


def stepwise(block, axis):
    return pl.BlockSpec(block, lambda i: tuple(i if d == axis else 0 for d in range(len(block))))


def after_core(keep, got, top, extra=0):
    end = keep.shape[1] - extra
    operands = [v.reshape((2, 2, 4) + v.shape[1:]) for v in (keep, got)]

    def fn(ins, outs):
        a_keep, a_send, b_keep, b_send = outs
        keep, got = ins
        for y in range(2):
            for x in range(2):
                total = add(keep[y, x, 0, :end], got[y, x, 0, :end]).astype(BF)
                (a_send if x else a_keep)[y, 0, :top, :] = total[:top]
                (b_send if y else b_keep)[x, 0, :, :] = total[top:]
        if extra:
            total = add(keep[0, 0, 0, end:], keep[0, 1, 0, end:]) + add(
                got[0, 0, 0, end:], got[0, 1, 0, end:]
            )
            for i, part in enumerate(in_pair(total)):
                for ref in (a_keep, a_send):
                    ref[i, 0, top:, :] = part

    dims = [(2, 4, top + extra, 128)] * 2 + [(2, 4, end - top, 128)] * 2
    return Additions(
        fn,
        tuple(operands),
        [stepwise((2, 2, 1) + v.shape[3:], 2) for v in operands],
        [stepwise((2, 1) + d[2:], 1) for d in dims],
        [shape(d, BF) for d in dims],
        4,
    )


def after_first(top, a_keep, a_got, b_keep, b_got):
    extra = a_keep.shape[2] - top

    def fn(ins, outs):
        a_keep, a_got, b_keep, b_got = ins
        a_next, a_send, b_next, b_send = outs
        for keep, got, stay, send in (
            (a_keep, a_got, a_next, a_send),
            (b_keep, b_got, b_next, b_send),
        ):
            n = stay.shape[1] if stay is b_next else top
            stay[0, :n] = add(keep[0, 0, :n], got[0, 0, :n]).astype(BF)
            send[0, :n] = add(keep[1, 0, :n], got[1, 0, :n]).astype(BF)
        if extra:
            total = add(a_keep[0, 0, top:], a_keep[1, 0, top:]) + add(
                a_got[0, 0, top:], a_got[1, 0, top:]
            )
            for i, part in enumerate(in_pair(total)):
                for ref in (a_next, a_send):
                    ref[0, top + i * extra : top + (i + 1) * extra] = part

    dims = [(4, top + 2 * extra, 128)] * 2 + [(4, b_keep.shape[2], 128)] * 2
    operands = (a_keep, a_got, b_keep, b_got)
    return Additions(
        fn,
        operands,
        [stepwise((2, 1) + v.shape[2:], 1) for v in operands],
        [stepwise((1,) + d[1:], 0) for d in dims],
        [shape(d, BF) for d in dims],
        4,
    )


def after_second_kernel(top, a_keep, a_got, b_keep, b_got, *outs):
    extra = (a_keep.shape[1] - top) // 2
    end = top + b_keep.shape[1]
    for i, ref in enumerate(outs):
        ref[:top] = add(a_keep[i, :top], a_got[i, :top]).astype(BF)
        ref[top:end] = add(b_keep[i], b_got[i]).astype(BF)
    if extra:
        for z in range(4):
            high, low = slice(top, top + extra), slice(top + extra, top + 2 * extra)
            total = add(a_keep[z, high], a_keep[z, low]) + add(a_got[z, high], a_got[z, low])
            for i, part in enumerate(in_pair(total)):
                at = end + (4 * i + z) * extra
                for ref in outs:
                    ref[at : at + extra] = part


def after_second(top, a_keep, a_got, b_keep, b_got):
    rows = top + b_keep.shape[1] + 4 * (a_keep.shape[1] - top)
    z = small(
        functools.partial(after_second_kernel, top),
        (a_keep, a_got, b_keep, b_got), [(rows, 128)] * 4,
    )
    return (z[0], *(flip(z[i], "narrow", 2 * i) for i in (1, 2, 3)))


def last_ff_kernel(z0, z1, z2, z3, w_out_ref, w_in_ref, sums_ref):
    out_rows, (height, width) = w_out_ref.shape[0], w_in_ref.shape
    total = add(z0[...], z1[...]) + add(z2[...], z3[...])
    w_out_ref[...] = total[:out_rows]
    for j in range(width // 128):
        at = out_rows + j * height
        w_in_ref[:, 128 * j : 128 * (j + 1)] = total[at : at + height]
    end = out_rows + height * width // 128
    rows = sums_ref.shape[0]
    sums_ref[...] = total[end : end + rows] + total[end + rows :]


def last_conv_kernel(z0, z1, z2, z3, out):
    out[...] = add(z0[...], z1[...]) + add(z2[...], z3[...])


def small(kernel, operands, dims, dtype=BF):
    moved = sum(v.size * v.dtype.itemsize for v in operands) * 2
    return pl.pallas_call(
        kernel,
        out_shape=[shape(d, dtype) for d in dims],
        compiler_params=params(12),
        cost_estimate=cost(moved / 2, moved),
        name="additions",
    )(*operands)


def after(value, *others):
    return lax.optimization_barrier((value, others))[0]


def body(
    inputs, conv_w, conv_b, ln1_gain, ln1_bias, w_in, b_in, w_out, ln2_gain, ln2_bias,
    segments, tap_mask, cotangent,
):
    rows, own, features = inputs.shape
    taps = conv_w.shape[0]
    reach = STEP * (taps // 2)
    hidden_units = w_in.shape[1]
    n_wide, n_narrow = lax.axis_size("wide"), lax.axis_size("narrow")
    by_hand = (n_wide, n_narrow) == (4, 8)
    blocks = (4, 8) if by_hand else (1, 1)

    near_pairs = [(i, i ^ 1) for i in range(n_wide)]
    far_pairs = [(i, i + 1 if i % 2 else i - 1) for i in range(1, n_wide - 1)]

    def exchange(near, far):
        far = lax.ppermute(far, "wide", far_pairs)
        return lax.ppermute(near, "wide", near_pairs), far

    def halos(value):
        ends = [
            lax.dynamic_slice_in_dim(value, side * (own - reach), reach, axis=1)
            for side in pair_sides()
        ]
        return exchange(*ends)

    in_place = functools.partial(pltpu.with_memory_space_constraint, memory_space=pltpu.HBM)
    *ends, info = pack(
        in_place(inputs), in_place(segments), in_place(jnp.transpose(tap_mask, (1, 0, 2))), reach
    )
    x_near, x_far = exchange(*ends)
    vec = jnp.stack([conv_b, ln1_gain, ln1_bias, ln2_gain, ln2_bias]).astype(F32)
    vec = jnp.pad(vec, ((0, 3), (0, 0)))

    acc = conv_inner(info, in_place(inputs), in_place(conv_w))
    hidden, info = conv_outer(info, acc, x_near, x_far, conv_w, vec)
    out, gmixed, gh, *grads = middle(
        blocks, hidden, inputs, cotangent, w_in, w_out, vec, b_in.astype(F32)[None]
    )
    if not by_hand:
        gh_near, gh_far = halos(gh)
        gconv = weight_gradient(blocks, info, gh, inputs, x_near, x_far, taps)
        gx = input_gradient(info, conv_w, gh, gh_near, gh_far, gmixed, 0, rows)

        def reduce(value, dims, wide_dim, narrow_dim):
            value = lax.psum_scatter(
                value.reshape(dims), "narrow", scatter_dimension=narrow_dim, tiled=True
            )
            return lax.psum_scatter(value, "wide", scatter_dimension=wide_dim, tiled=True).astype(
                F32
            )

        grad_w_out = reduce(grads[0], (hidden_units, features), 1, 0)
        grad_w_in = reduce(grads[1], (features, hidden_units), 1, 0)
        grad_conv = reduce(gconv[0], (taps, features, features), 2, 1)
        sums = lax.psum(grads[2], ("wide", "narrow"))
    else:
        together = lax.optimization_barrier
        cuts = (0, (3 * rows + 4) // 8, rows - rows // 4, rows)

        def inputs_part(i, gx):
            first, end = cuts[i], cuts[i + 1]
            return input_gradient(info, conv_w, gh, gh_near, gh_far, gx, first, end - first)

        height = features // n_narrow
        f_top = (grads[0].shape[1] - 16) * 11 // 16 // 16 * 16
        c_top = taps * height // 2 // 16 * 16
        f_got = flip(grads[1], "wide", 1)
        gh_near, gh_far = halos(gh)
        f = alone(after_core(grads[0], f_got, f_top, 16))
        f_got = flip(f[1], "narrow", 1), flip(f[3], "wide", 2)
        c = weight_gradient(blocks, info, after(gh, *f), in_place(inputs), in_place(x_near), in_place(x_far), taps)

        c, f, f_got, gh_near, gh_far = together((c, f, f_got, gh_near, gh_far))
        c_got = flip(c[1], "wide", 1)
        f = alone(after_first(f_top, f[0], f_got[0], f[2], f_got[1]))
        f_got = flip(f[1], "wide", 2), flip(f[3], "narrow", 1)
        gx = inputs_part(0, after(gmixed, *f))

        gx, c, c_got, f, f_got = together((gx, c[0], c_got, f, f_got))
        c = alone(after_core(c, c_got, c_top))
        c_got = flip(c[1], "narrow", 1), flip(c[3], "wide", 2)
        f = after_second(f_top, *after((f[0], f_got[0], f[2], f_got[1]), *c))
        gx = inputs_part(1, after(gx, *c, f[0]))

        gx, c, c_got, f = together((gx, c, c_got, f))
        c = alone(after_first(c_top, c[0], c_got[0], c[2], c_got[1]))
        c_got = flip(c[1], "wide", 2), flip(c[3], "narrow", 1)
        gx = inputs_part(2, after(gx, *c))

        gx, c, c_got, f = together((gx, c, c_got, f))
        c = after_second(c_top, c[0], c_got[0], c[2], c_got[1])
        f = after(f, c[0])
        grad_w_out, grad_w_in, sums = small(
            last_ff_kernel, f,
            [(hidden_units // n_narrow, 128), (height, hidden_units // n_wide), (64, 128)],
            F32,
        )
        grad_conv = small(last_conv_kernel, c, [(taps * height, 128)], F32)[0]
        grad_conv = grad_conv.reshape(taps, height, features // n_wide)
    sums = sums.reshape(-1)
    starts = [0, features, 2 * features, 3 * features]
    starts += [starts[-1] + hidden_units, starts[-1] + hidden_units + features]
    sizes = [features, features, features, hidden_units, features, features]
    vectors = [sums[a : a + n] for a, n in zip(starts, sizes, strict=True)]
    return (
        out, gx, grad_conv, vectors[0], vectors[1], vectors[2], grad_w_in, vectors[3],
        grad_w_out, vectors[4], vectors[5],
    )


def solution(mesh):
    split = P("narrow", "wide", None)
    placed = (split,) + (P(),) * 9 + (P("narrow", "wide"), P("narrow", None, "wide"), split)
    return jax.shard_map(
        body,
        mesh=mesh,
        in_specs=placed,
        out_specs=(
            split, split, P(None, "narrow", "wide"), P(), P(), P(), P("narrow", "wide"), P(),
            P("narrow", "wide"), P(), P(),
        ),
        check_vma=False,
    )
```
